32 devices in a mesh: members: 2 (over x), lon: 8 (over z, y), lat: 2 (over core).
Axes of the slice: x: 2, y: 2, z: 4, core: 2. Of those that a mesh axis runs over, the one named last changes fastest.
Arguments:
- ocean_state: bfloat16 [200, 128, 1024], P(None, ('members', 'lat'), 'lon'), parts along dimension 1
- cotangent: bfloat16 [200, 128, 1024], P(None, ('members', 'lat'), 'lon'), parts along dimension 1
- kernel: float32 [200, 49], replicated, may hold values from -0.875 to 0.875
- norm_gain: float32 [200], replicated, may hold values from 0.1 to 1.9
- expand_weight: bfloat16 [200, 800], replicated, may hold values from -0.4375 to 0.4375
- reduce_weight: bfloat16 [800, 200], replicated, may hold values from -0.21875 to 0.21875
- layer_scale: float32 [200], replicated, may hold values from 0.5 to 1.5
- land_mask: int32 [64, 1024], P('lat', 'lon'), may hold values 0 or 1
Outputs:
- block_out: bfloat16 [200, 128, 1024], P(None, ('members', 'lat'), 'lon'), parts along dimension 1
- state_grad: bfloat16 [200, 128, 1024], P(None, ('members', 'lat'), 'lon'), parts along dimension 1
- kernel_grad: float32 [400, 49], P('members'), parts along dimension 0
- gain_grad: float32 [400], P('members'), parts along dimension 0
- expand_grad: float32 [400, 800], P('members'), parts along dimension 0
- reduce_grad: float32 [1600, 200], P('members'), parts along dimension 0
- scale_grad: float32 [400], P('members'), parts along dimension 0
The draws below stay inside these ranges and needn't reach their ends.
There are 2 independent parts, one for each index of `members`. The reference program is written for one: setup_inputs(seed, part) draws one part's arguments, and reference() takes and returns one part's arrays. A program takes and returns all parts, laid end to end along the dimension named above; an argument that names none is the same for every part. Nothing has to cross between parts.
All inputs are finite; a program needn't handle non-finite values. No bound on the sum of `land_mask` on one device may be relied on, other than what follows from the above.
Results may differ from the reference program's by a relative error of at most 0.0065.
Values may be sent and summed in bfloat16 or wider, within the bound.
No kernel may reach another device: no remote copies, remote signals or barrier semaphores. Data moves between devices by JAX's collectives and lax.ppermute only.
A program may use at most 448 MiB of HBM per device.

```python
import math
import jax
import jax.numpy as jnp
from jax import lax

C = 200
FF = 800
KS = 7
ROWS = 64
LON = 1024


def draw_ocean_state(key, part):
    key_scale, key_base = jax.random.split(key, 2)
    spread = jnp.exp(jax.random.uniform(key_scale, (C, 1, 1), jnp.float32, 0.0, math.log(10.0))) / 3.0
    base = jax.random.normal(key_base, (C, ROWS, LON), jnp.float32)
    return (spread * base).astype(jnp.bfloat16)


def draw_cotangent(key, part):
    ramp = 1.0 + 2.0 * jnp.arange(LON, dtype=jnp.float32) / (LON - 1)
    base = jax.random.normal(key, (C, ROWS, LON), jnp.float32)
    return (base * ramp[None, None, :]).astype(jnp.bfloat16)


def set_ends(array, stream_key, low, largest):
    dims = array.shape
    spot = [jax.random.randint(jax.random.fold_in(stream_key, axis), (), 0, dims[axis]) for axis in range(len(dims))]
    array = array.at[tuple(spot)].set(low)
    longest = dims.index(max(dims))
    spot[longest] = (spot[longest] + 1) % dims[longest]
    return array.at[tuple(spot)].set(largest)


def normal_values(own_key, extent, width, most, held_as=jnp.bfloat16):
    result = jax.random.normal(own_key, extent, jnp.float32) * width
    return jnp.minimum(jnp.maximum(result, -most), most).astype(held_as)


def setup_inputs(seed: int = 0, part: int = 0) -> dict:
    splits = jax.random.split(jax.random.key(seed), 9)
    part_keys = jax.random.split(jax.random.fold_in(splits[8], part), 9)
    ocean_state = draw_ocean_state(jax.random.fold_in(jax.random.fold_in(splits[8], part), 71), part)
    cotangent = draw_cotangent(jax.random.fold_in(jax.random.fold_in(splits[8], part), 71), part)
    kernel = normal_values(splits[2], (C, KS * KS), (KS * KS) ** -0.5, 0.875, jnp.float32)
    norm_gain = jnp.clip(1.0 + 0.18 * jax.random.normal(splits[3], (C,), jnp.float32), 0.1, 1.9)
    expand_weight = normal_values(splits[4], (C, FF), C ** -0.5, 0.4375)
    reduce_weight = normal_values(splits[5], (FF, C), FF ** -0.5, 0.21875)
    layer_scale = jnp.clip(jax.random.uniform(splits[6], (C,), jnp.float32, 0.5, 1.5), 0.5, 1.5)
    land_mask = set_ends((jax.random.randint(splits[7], (ROWS, LON), 0, 4) < 3).astype(jnp.int32), jax.random.fold_in(splits[7], 1), 0, 1)
    return {"ocean_state": ocean_state, "cotangent": cotangent, "kernel": kernel, "norm_gain": norm_gain, "expand_weight": expand_weight, "reduce_weight": reduce_weight, "layer_scale": layer_scale, "land_mask": land_mask}


def gelu(value):
    return jax.nn.gelu(value, approximate=True)

def extend(field):
    channels, height, breadth = field.shape
    reach = KS // 2
    wrapped = jnp.concatenate([field[:, :, breadth - reach:], field, field[:, :, :reach]], axis=2)
    columns = (breadth - 1 - jnp.mod(jnp.arange(breadth + 2 * reach) - reach, breadth)).astype(jnp.int32)
    north = jnp.take(field[:, height - 1 - jnp.arange(reach)], columns, axis=2)
    south = jnp.zeros((channels, reach, breadth + 2 * reach), field.dtype)
    return (jnp.concatenate([south, wrapped, north], axis=1), columns)

def reference(ocean_state, cotangent, kernel, norm_gain, expand_weight, reduce_weight, layer_scale, land_mask):
    channels, height, breadth = ocean_state.shape
    reach = KS // 2
    statef = ocean_state.astype(jnp.float32)
    extended, columns = extend(statef)
    convolved = jnp.zeros((channels, height, breadth), jnp.float32)
    for row_shift in range(KS):
        for col_shift in range(KS):
            tap_weight = kernel[:, row_shift * KS + col_shift][:, None, None]
            convolved = convolved + tap_weight * extended[:, row_shift:row_shift + height, col_shift:col_shift + breadth]
    average = lax.optimization_barrier(jnp.mean(convolved, axis=0))
    centred = convolved - average
    variance = lax.optimization_barrier(jnp.mean(centred * centred, axis=0))
    inverse = lax.rsqrt(variance + 1e-06)
    normalized = centred * inverse
    normed = (normalized * norm_gain[:, None, None]).astype(jnp.bfloat16)
    wet_cells = land_mask.astype(jnp.float32)
    branch_grad = cotangent.astype(jnp.float32) * wet_cells[None]

    def row_pass(carry, items):
        expand_acc, reduce_acc = carry
        normed_row, grad_row = items
        hidden = jnp.dot(expand_weight.T, normed_row, preferred_element_type=jnp.float32)
        activated = gelu(hidden).astype(jnp.bfloat16)
        mixed = jnp.dot(reduce_weight.T, activated, preferred_element_type=jnp.float32)
        mixed_grad = (layer_scale[:, None] * grad_row).astype(jnp.bfloat16)
        reduce_acc = reduce_acc + jnp.dot(activated, mixed_grad.T, preferred_element_type=jnp.float32)
        act_grad = jnp.dot(reduce_weight, mixed_grad, preferred_element_type=jnp.float32)
        pullback = jax.vjp(gelu, hidden)[1]
        hidden_grad = pullback(act_grad)[0].astype(jnp.bfloat16)
        expand_acc = expand_acc + jnp.dot(normed_row, hidden_grad.T, preferred_element_type=jnp.float32)
        normed_grad = jnp.dot(expand_weight, hidden_grad, preferred_element_type=jnp.float32)
        return ((expand_acc, reduce_acc), (mixed, normed_grad))
    start = (jnp.zeros((channels, FF), jnp.float32), jnp.zeros((FF, channels), jnp.float32))
    (expand_grad, reduce_grad), (mixed_rows, normed_rows) = lax.scan(row_pass, start, (jnp.transpose(normed, (1, 0, 2)), jnp.transpose(branch_grad, (1, 0, 2))))
    mixed = jnp.transpose(mixed_rows, (1, 0, 2))
    normed_grad = jnp.transpose(normed_rows, (1, 0, 2))
    block_out = (statef + wet_cells[None] * layer_scale[:, None, None] * mixed).astype(jnp.bfloat16)
    scale_grad = lax.optimization_barrier(jnp.sum(branch_grad * mixed, axis=(1, 2)))
    gain_grad = lax.optimization_barrier(jnp.sum(normed_grad * normalized, axis=(1, 2)))
    unit_grad = normed_grad * norm_gain[:, None, None]
    conv_grad = (inverse * (unit_grad - lax.optimization_barrier(jnp.mean(unit_grad, axis=0)) - normalized * lax.optimization_barrier(jnp.mean(unit_grad * normalized, axis=0)))).astype(jnp.bfloat16)
    conv_wide = conv_grad.astype(jnp.float32)
    kernel_terms = []
    padded_grad = jnp.zeros((channels, height + 2 * reach, breadth + 2 * reach), jnp.float32)
    for row_shift in range(KS):
        for col_shift in range(KS):
            tap_weight = kernel[:, row_shift * KS + col_shift][:, None, None]
            window = extended[:, row_shift:row_shift + height, col_shift:col_shift + breadth]
            kernel_terms.append(lax.optimization_barrier(jnp.sum(conv_wide * window, axis=(1, 2))))
            padded_grad = padded_grad + jnp.pad(tap_weight * conv_wide, ((0, 0), (row_shift, 2 * reach - row_shift), (col_shift, 2 * reach - col_shift)))
    kernel_grad = jnp.stack(kernel_terms, axis=1)
    middle = padded_grad[:, reach:height + reach]
    inner = middle[:, :, reach:breadth + reach]
    inner = inner.at[:, :, :reach].add(middle[:, :, breadth + reach:])
    inner = inner.at[:, :, breadth - reach:].add(middle[:, :, :reach])
    fold_part = padded_grad[:, height + reach:]
    fold_rows = (height - 1 - jnp.arange(reach)).astype(jnp.int32)
    inner = inner.at[:, fold_rows[:, None], columns[None, :]].add(fold_part)
    state_grad = (cotangent.astype(jnp.float32) + inner).astype(jnp.bfloat16)
    return (block_out, state_grad, kernel_grad, gain_grad, expand_grad, reduce_grad, scale_grad)
```

```python
import jax
import jax.numpy as jnp
from jax import lax
from jax.experimental import pallas as pl
from jax.experimental.pallas import tpu as pltpu
from jax.sharding import PartitionSpec as P

KS = 7
REACH = KS // 2
F32 = jnp.float32
BF16 = jnp.bfloat16
HALO = 8
VMEM_LIMIT = 58 << 20


def vmem():
    return pl.BlockSpec(memory_space=pltpu.VMEM)


def smem():
    return pl.BlockSpec(memory_space=pltpu.SMEM)


def call(body, outs, scratch=(), n_smem=0, n_in=0, cost=None):
    return pl.pallas_call(
        body,
        out_shape=outs,
        in_specs=[smem()] * n_smem + [vmem()] * (n_in - n_smem),
        out_specs=jax.tree.map(lambda _: vmem(), outs),
        scratch_shapes=list(scratch),
        compiler_params=pltpu.CompilerParams(vmem_limit_bytes=VMEM_LIMIT),
        cost_estimate=cost,
    )


def dot(a, b, ca, cb):
    return lax.dot_general(a, b, (((ca,), (cb,)), ((), ())), preferred_element_type=F32)


def shape(dims, dtype):
    return jax.ShapeDtypeStruct(dims, dtype)


def iota(dims, axis):
    return lax.broadcasted_iota(jnp.int32, dims, axis)


def as_f32(mask):
    return jnp.where(mask, 1.0, 0.0).astype(F32)


def tap_rows(rows):
    total = KS * (rows + HALO) + HALO
    q = iota((rows, total), 1)
    r = iota((rows, total), 0)
    t = (q - KS * rows) % HALO
    halo = jnp.where(t < REACH, rows + t, jnp.where(t < 2 * REACH, t - 2 * REACH, 4 * rows))
    halo = jnp.where(q < KS * (rows + HALO), halo, 4 * rows)
    return jnp.where(q < KS * rows, q % rows, halo) - r


def shift_stack(own, edge):
    lanes = own.shape[1]
    rows = own.shape[0] - HALO
    lane = iota(own.shape, 1)
    mains, halos = [], []
    for j in range(KS):
        d = j - REACH
        if d == 0:
            s = own
        elif d > 0:
            s = pltpu.roll(jnp.where(lane < d, edge, own), lanes - d, 1)
        else:
            s = pltpu.roll(jnp.where(lane >= lanes + d, edge, own), -d, 1)
        mains.append(s[:rows].astype(BF16))
        halos.append(s[rows:])
    halos.append(jnp.zeros_like(halos[0]))
    pairs = [
        jnp.concatenate([halos[i], halos[i + 1]], axis=0).astype(BF16)
        for i in range(0, KS + 1, 2)
    ]
    return jnp.concatenate(mains + pairs, axis=0)


def stage_halo(north, lat_ref, fold_ref, rb, rh):
    channels, lanes = lat_ref.shape[1], lat_ref.shape[2] // 2
    is_north = north != 0
    for t in range(REACH):
        near = lat_ref[t].astype(F32)
        far = fold_ref[t].astype(F32)
        up = jnp.where(is_north, far, near)
        low = jnp.where(is_north, near, jnp.zeros_like(near))
        rb[pl.ds(t * channels, channels), :] = up[:, :lanes]
        rh[pl.ds(t * channels, channels), :] = up[:, lanes:]
        rb[pl.ds((REACH + t) * channels, channels), :] = low[:, :lanes]
        rh[pl.ds((REACH + t) * channels, channels), :] = low[:, lanes:]
    for t in range(2 * REACH, HALO):
        rb[pl.ds(t * channels, channels), :] = jnp.zeros((channels, lanes), F32)
        rh[pl.ds(t * channels, channels), :] = jnp.zeros((channels, lanes), F32)


def channel_stack(c, channels, x_ref, h_ref, rb, rh):
    own = jnp.concatenate([x_ref[c].astype(F32), rb[pl.ds(c, HALO, stride=channels), :]], axis=0)
    edge = jnp.concatenate([h_ref[c].astype(F32), rh[pl.ds(c, HALO, stride=channels), :]], axis=0)
    return shift_stack(own, edge)


def pack_kernel(x_ref, lo_ref, hi_ref):
    lanes = x_ref.shape[1]
    k = iota((2 * HALO, lanes), 0)
    lane = iota((2 * HALO, lanes), 1)
    pick = ((k < REACH) & (lane == k)) | (
        (k >= HALO) & (k < HALO + REACH) & (lane == lanes - REACH + k - HALO)
    )
    sel = as_f32(pick).astype(BF16)
    edges = dot(sel, x_ref[...], 1, 1)
    lo_ref[...] = edges[:HALO].astype(BF16)
    hi_ref[...] = edges[HALO:].astype(BF16)


def unpack_kernel(north_ref, x_ref, east_ref, west_ref, h_ref, lat_ref, fold_ref, xs, hs):
    channels, rows, lanes = x_ref.shape
    k = iota((HALO, lanes), 0)
    lane = iota((HALO, lanes), 1)
    sel_e = as_f32((k < REACH) & (lane == k)).astype(BF16)
    sel_w = as_f32((k < REACH) & (lane == lanes - REACH + k)).astype(BF16)
    sel = jnp.concatenate([sel_e, sel_w], axis=0)
    ed = jnp.concatenate([east_ref[...], west_ref[...]], axis=0)
    hf = dot(ed, sel, 0, 0).reshape(channels, rows, lanes)
    h_ref[...] = hf.astype(BF16)
    g = HALO
    xs[0] = x_ref[:, :16, :].astype(F32)[:, :g].reshape(channels * g, lanes)
    xs[1] = x_ref[:, rows - 16 :, :].astype(F32)[:, 16 - g :].reshape(channels * g, lanes)
    hs[0] = hf[:, :g].reshape(channels * g, lanes)
    hs[1] = hf[:, rows - g :].reshape(channels * g, lanes)
    is_north = north_ref[0] != 0
    rev = as_f32(iota((lanes, lanes), 0) + iota((lanes, lanes), 1) == lanes - 1).astype(BF16)
    for t in range(REACH):
        for part, ref in ((0, xs), (1, hs)):
            bottom = ref.at[0][pl.ds(t, channels, stride=g), :]
            top = ref.at[1][pl.ds(g - REACH + t, channels, stride=g), :]
            span = slice(part * lanes, (part + 1) * lanes)
            lat_ref[t, :, span] = jnp.where(is_north, bottom, top).astype(BF16)
            fold_ref[REACH - 1 - t, :, span] = dot(top.astype(BF16), rev, 1, 0).astype(BF16)


def table_kernel(tab_ref, tab2_ref, a_ref, a2_ref):
    channels, rows, total = a_ref.shape
    gap = tap_rows(rows)

    def step(c, carry):
        one = jnp.zeros((rows, total), F32)
        two = jnp.zeros((rows, total), F32)
        for a in range(KS):
            hit = gap == a - REACH
            one = jnp.where(hit, tab_ref[c, a : a + 1, :], one)
            two = jnp.where(hit, tab2_ref[c, a : a + 1, :], two)
        a_ref[c] = one.astype(BF16)
        a2_ref[c] = two.astype(BF16)
        return carry

    lax.fori_loop(0, channels, step, 0)


def gelu_parts(hidden):
    k0 = 0.7978845608028654
    k1 = 0.044715 * k0
    sq = hidden * hidden
    th = jnp.tanh(hidden * (k0 + k1 * sq))
    half = 0.5 * th + 0.5
    act = hidden * half
    slope = half + act * (1.0 - th) * (k0 + 3.0 * k1 * sq)
    return act, slope


def main_kernel(
    north_ref, x_ref, h_ref, lat_ref, fold_ref, a_ref, cot_ref, mask_ref, gain_ref, scale_ref,
    wet_ref, we_ref, wr_ref, wrt_ref,
    out_ref, g_ref, exp_ref, red_ref, sums_ref,
    conv, cots, gs, ms, rb, rh, act_s, hg_s,
):
    channels, rows, lanes = x_ref.shape
    hiddens = we_ref.shape[1]
    stage_halo(north_ref[0], lat_ref, fold_ref, rb, rh)

    def conv_step(c, carry):
        stack = channel_stack(c, channels, x_ref, h_ref, rb, rh)
        conv[pl.ds(c, rows, stride=channels), :] = dot(a_ref[c], stack, 1, 0)
        cots[pl.ds(c, rows, stride=channels), :] = cot_ref[c].astype(F32) * mask_ref[...]
        return carry

    lax.fori_loop(0, channels, conv_step, 0, unroll=2)
    exp_ref[...] = jnp.zeros_like(exp_ref)
    red_ref[...] = jnp.zeros_like(red_ref)
    sums_ref[...] = jnp.zeros_like(sums_ref)

    def pair(ref, i):
        first = pl.multiple_of(2 * i * channels, 8)
        second = pl.multiple_of((2 * i + 1) * channels, 8)
        return jnp.concatenate(
            [ref[pl.ds(first, channels), :], ref[pl.ds(second, channels), :]], axis=1
        )

    def unpair(ref, i, value):
        ref[pl.ds(2 * i, channels, stride=rows), :] = value[:, :lanes]
        ref[pl.ds(2 * i + 1, channels, stride=rows), :] = value[:, lanes:]

    def cell_step(i, carry):
        gain = gain_ref[...]
        scale = scale_ref[...]
        value = pair(conv, i)
        centred = value - jnp.mean(value, axis=0, keepdims=True)
        inverse = lax.rsqrt(jnp.mean(centred * centred, axis=0, keepdims=True) + 1e-06)
        normalized = centred * inverse
        normed = (normalized * gain).astype(BF16)
        branch = pair(cots, i)
        mixed_grad = (scale * branch).astype(BF16)
        part = 160
        for f in range(0, hiddens, part):
            hidden = dot(wet_ref[f : f + part, :], normed, 1, 0)
            act_grad = dot(wr_ref[f : f + part, :], mixed_grad, 1, 0)
            act, slope = gelu_parts(hidden)
            act_s[f : f + part, :] = act.astype(BF16)
            hg_s[f : f + part, :] = (act_grad * slope).astype(BF16)
        mixed = dot(wrt_ref[...], act_s[...], 1, 0)
        red_ref[...] += dot(act_s[...], mixed_grad, 1, 1)
        normed_grad = dot(we_ref[...], hg_s[...], 1, 0)
        exp_ref[...] += dot(hg_s[...], normed, 1, 1)
        unpair(ms, i, scale * mixed)
        scaled = branch * mixed
        sums_ref[1] += scaled[:, :lanes] + scaled[:, lanes:]
        gained = normed_grad * normalized
        sums_ref[0] += gained[:, :lanes] + gained[:, lanes:]
        unit = normed_grad * gain
        m1 = jnp.mean(unit, axis=0, keepdims=True)
        m2 = jnp.mean(unit * normalized, axis=0, keepdims=True)
        unpair(gs, i, inverse * (unit - m1 - normalized * m2))
        return carry

    lax.fori_loop(0, rows // 2, cell_step, 0)

    def out_step(c, carry):
        at = pl.multiple_of(c * rows, rows)
        out_ref[c] = (x_ref[c].astype(F32) + mask_ref[...] * ms[pl.ds(at, rows), :]).astype(BF16)
        g_ref[c] = gs[pl.ds(at, rows), :].astype(BF16)
        return carry

    lax.fori_loop(0, channels, out_step, 0, unroll=4)


def tap_kernel(north_ref, x_ref, h_ref, lat_ref, fold_ref, g_ref, kg_ref, rb, rh, rowsum):
    channels, rows, lanes = x_ref.shape
    total = KS * (rows + HALO) + HALO
    stage_halo(north_ref[0], lat_ref, fold_ref, rb, rh)
    gap = tap_rows(rows)

    def step(c, carry):
        stack = channel_stack(c, channels, x_ref, h_ref, rb, rh)
        m = dot(g_ref[c], stack, 1, 1)
        for a in range(KS):
            rowsum[a, pl.ds(c, 1), :] = jnp.sum(
                jnp.where(gap == a - REACH, m, 0.0), axis=0, keepdims=True
            )
        return carry

    lax.fori_loop(0, channels, step, 0, unroll=2)
    q = iota((total, lanes), 0)
    block = jnp.where(q < KS * rows, q // rows, (q - KS * rows) // HALO)
    group = as_f32(block == iota((total, lanes), 1)).astype(BF16)
    for a in range(KS):
        v = rowsum[a]
        hi = v.astype(BF16)
        lo = (v - hi.astype(F32)).astype(BF16)
        kg_ref[a] = dot(hi, group, 1, 0) + dot(lo, group, 1, 0)


def adjoint_kernel(north_ref, g_ref, h_ref, lat_ref, fold_ref, a_ref, cot_ref, out_ref, rb, rh):
    channels, rows, lanes = g_ref.shape
    stage_halo(north_ref[0], lat_ref, fold_ref, rb, rh)

    def step(c, carry):
        stack = channel_stack(c, channels, g_ref, h_ref, rb, rh)
        out_ref[c] = (cot_ref[c].astype(F32) + dot(a_ref[c], stack, 1, 0)).astype(BF16)
        return carry

    lax.fori_loop(0, channels, step, 0, unroll=2)


def halo_exchange(field, north):
    channels, rows, lanes = field.shape
    n, m = lax.axis_size("lon"), lax.axis_size("lat")
    edge = shape((HALO, channels * rows), BF16)
    low, high = call(pack_kernel, (edge, edge), n_in=1)(field.reshape(channels * rows, lanes))
    from_east = lax.ppermute(low, "lon", [((i + 1) % n, i) for i in range(n)])
    from_west = lax.ppermute(high, "lon", [(i, (i + 1) % n) for i in range(n)])
    msg = shape((REACH, channels, 2 * lanes), BF16)
    lane_halo, lat_msg, fold_msg = call(
        unpack_kernel,
        (shape(field.shape, BF16), msg, msg),
        scratch=[pltpu.VMEM((2, channels * HALO, lanes), F32)] * 2,
        n_smem=1,
        n_in=4,
    )(north, field, from_east, from_west)
    lat_rows = lax.ppermute(lat_msg, "lat", [(0, 1), (1, 0)])
    fold_rows = lax.ppermute(
        fold_msg, ("lon", "lat"), [(i * m + m - 1, (n - 1 - i) * m + m - 1) for i in range(n)]
    )
    return lane_halo, lat_rows, fold_rows


def split_half(buf, bit):
    rows, lanes = buf.shape
    if (rows // 2) % 8 and lanes > 128:
        first, second = buf[:, : lanes // 2], buf[:, lanes // 2 :]
    else:
        first, second = buf[: rows // 2], buf[rows // 2 :]
    up = bit != 0
    return jnp.where(up, second, first), jnp.where(up, first, second)


def join_half(mine, other, bit, dims):
    up = bit != 0
    first, second = jnp.where(up, other, mine), jnp.where(up, mine, other)
    return jnp.concatenate([first, second], axis=1 if mine.shape[0] == dims[0] else 0)


def all_sum(buf):
    steps = [("lat", 0)] + [("lon", b) for b in range(lax.axis_size("lon").bit_length() - 1)]
    sizes = []
    for axis, b in steps:
        bit = (lax.axis_index(axis) >> b) & 1
        sizes.append(buf.shape)
        keep, send = split_half(buf, bit)
        pairs = [(i, i ^ (1 << b)) for i in range(lax.axis_size(axis))]
        buf = keep + lax.ppermute(send.astype(BF16), axis, pairs).astype(F32)
    buf = buf.astype(BF16)
    for (axis, b), dims in zip(steps[::-1], sizes[::-1]):
        bit = (lax.axis_index(axis) >> b) & 1
        pairs = [(i, i ^ (1 << b)) for i in range(lax.axis_size(axis))]
        buf = join_half(buf, lax.ppermute(buf, axis, pairs), bit, dims)
    return buf.astype(F32)


def stack_taps(taps, halo_taps, rows):
    main = jnp.repeat(taps, rows, axis=2)
    halo = jnp.concatenate([jnp.repeat(t[:, :, :, None], n, axis=3) for t, n in halo_taps], axis=3)
    halo = halo.reshape(taps.shape[0], KS, KS * HALO)
    both = jnp.concatenate([main, halo], axis=2)
    return jnp.pad(both, ((0, 0), (0, 1), (0, HALO)))


def on_device(
    ocean_state, cotangent, kernel, norm_gain, expand_weight, reduce_weight, layer_scale, land_mask
):
    channels, rows, lanes = ocean_state.shape
    hiddens = expand_weight.shape[1]
    total = KS * (rows + HALO) + HALO
    is_north = lax.axis_index("lat") == lax.axis_size("lat") - 1
    north = is_north.astype(jnp.int32).reshape(1)
    mask = land_mask.astype(F32)

    halo, lat_rows, fold_rows = halo_exchange(ocean_state, north)

    taps = kernel.reshape(channels, KS, KS)
    flipped = taps[:, ::-1, ::-1]
    beyond = jnp.where(is_north, taps, flipped)
    tab = stack_taps(taps, ((taps, HALO),), rows)
    tab2 = stack_taps(flipped, ((beyond, REACH), (flipped, HALO - REACH)), rows)
    table = shape((channels, rows, total), BF16)
    forward_table, adjoint_table = call(table_kernel, (table, table), n_in=2)(tab, tab2)

    rowbuf = pltpu.VMEM((HALO * channels, lanes), F32)
    cellbuf = pltpu.VMEM((channels * rows, lanes), F32)
    field = shape(ocean_state.shape, BF16)
    block_out, conv_grad, exp_part, red_part, sums = call(
        main_kernel,
        (
            field,
            field,
            shape((hiddens, channels), F32),
            shape((hiddens, channels), F32),
            shape((2, channels, lanes), F32),
        ),
        scratch=[cellbuf] * 4 + [rowbuf] * 2 + [pltpu.VMEM((hiddens, 2 * lanes), BF16)] * 2,
        n_smem=1,
        n_in=14,
    )(
        north, ocean_state, halo, lat_rows, fold_rows, forward_table, cotangent, mask,
        norm_gain.reshape(channels, 1), layer_scale.reshape(channels, 1),
        expand_weight.T, expand_weight, reduce_weight, reduce_weight.T,
    )

    g_halo, g_lat, g_fold = halo_exchange(conv_grad, north)

    kg = call(
        tap_kernel,
        shape((KS, channels, lanes), F32),
        scratch=[rowbuf] * 2 + [pltpu.VMEM((KS, channels, total), F32)],
        n_smem=1,
        n_in=6,
    )(north, ocean_state, halo, lat_rows, fold_rows, conv_grad)

    state_grad = call(
        adjoint_kernel, field, scratch=[rowbuf] * 2, n_smem=1, n_in=7
    )(north, conv_grad, g_halo, g_lat, g_fold, adjoint_table, cotangent)

    kernel_part = jnp.transpose(kg[:, :, :KS], (1, 0, 2)).reshape(channels, KS * KS)
    small = jnp.concatenate(
        [kernel_part, jnp.sum(sums[0], axis=1)[:, None], jnp.sum(sums[1], axis=1)[:, None]], axis=1
    )
    spare = 256 - channels
    small = jnp.pad(small, ((0, 2 * hiddens - channels), (0, spare - small.shape[1])))
    buf = jnp.concatenate([jnp.concatenate([exp_part, red_part], axis=0), small], axis=1)
    buf = all_sum(buf)
    expand_grad = buf[:hiddens, :channels].T
    reduce_grad = buf[hiddens:, :channels]
    tail = buf[:channels, channels:]
    kernel_grad = tail[:, : KS * KS]
    gain_grad = tail[:, KS * KS]
    scale_grad = tail[:, KS * KS + 1]
    return (block_out, state_grad, kernel_grad, gain_grad, expand_grad, reduce_grad, scale_grad)


def solution(mesh):
    tiles = P(None, ("members", "lat"), "lon")
    return jax.shard_map(
        on_device,
        mesh=mesh,
        in_specs=(tiles, tiles, P(), P(), P(), P(), P(), P("lat", "lon")),
        out_specs=(
            tiles, tiles, P("members", None), P("members"), P("members", None),
            P("members", None), P("members"),
        ),
        check_vma=False,
    )
```

```python
import functools

import jax
import jax.numpy as jnp
from jax import lax
from jax.experimental import pallas as pl
from jax.experimental.pallas import tpu as pltpu
from jax.sharding import PartitionSpec as P

KS = 7
REACH = KS // 2
F32 = jnp.float32
BF16 = jnp.bfloat16
HALO = 8
VMEM_LIMIT = 58 << 20
CHUNKS = 5


def vmem():
    return pl.BlockSpec(memory_space=pltpu.VMEM)


def smem():
    return pl.BlockSpec(memory_space=pltpu.SMEM)


def call(body, outs, scratch=(), n_smem=0, n_in=0, cost=None):
    return pl.pallas_call(
        body,
        out_shape=outs,
        in_specs=[smem()] * n_smem + [vmem()] * (n_in - n_smem),
        out_specs=jax.tree.map(lambda _: vmem(), outs),
        scratch_shapes=list(scratch),
        compiler_params=pltpu.CompilerParams(vmem_limit_bytes=VMEM_LIMIT),
        cost_estimate=cost,
    )


def grid_call(body, grid, outs, in_specs, out_specs, scratch, cost, aliases=None):
    return pl.pallas_call(
        body,
        grid=(grid,),
        out_shape=outs,
        in_specs=in_specs,
        out_specs=out_specs,
        scratch_shapes=list(scratch),
        input_output_aliases=aliases or {},
        compiler_params=pltpu.CompilerParams(
            vmem_limit_bytes=VMEM_LIMIT, dimension_semantics=("arbitrary",)
        ),
        cost_estimate=cost,
    )


def dot(a, b, ca, cb):
    return lax.dot_general(a, b, (((ca,), (cb,)), ((), ())), preferred_element_type=F32)


def shape(dims, dtype):
    return jax.ShapeDtypeStruct(dims, dtype)


def iota(dims, axis):
    return lax.broadcasted_iota(jnp.int32, dims, axis)


def as_f32(mask):
    return jnp.where(mask, 1.0, 0.0).astype(F32)


def stack_base(rows):
    return (KS + 1) * rows


def tap_places(rows):
    width = stack_base(rows) + 256
    q = iota((KS * KS, width), 1)
    base = stack_base(rows)
    w = q % 128 + REACH
    w = jnp.where(w >= 128, w - 128, w)
    row_j = q // 128 * (128 // rows) + w // rows
    row_a = w % rows
    t = q % HALO
    halo_j = (q - base) % 128 // HALO
    upper = q >= base + 128
    halo_a = jnp.where(upper, t + REACH + 1, t - REACH)
    j = jnp.where(q < base, row_j, halo_j)
    a = jnp.where(q < base, row_a, halo_a)
    halo_ok = (upper & (t < REACH)) | ((q < base + 128) & (t >= REACH) & (t < 2 * REACH))
    ok = (j < KS) & (a < KS) & (a >= 0) & ((q < base) | halo_ok)
    return jnp.where(ok, a * KS + j, -1), upper


def split(value):
    high = value.astype(BF16)
    return high, (value - high.astype(F32)).astype(BF16)


def tap_rows(taps, rows, adjoint=None):
    place, upper = tap_places(rows)
    if adjoint is not None:
        keep = (upper & (adjoint != 0)) | (place < 0)
        place = jnp.where(keep, place, KS * KS - 1 - place)
    pick = as_f32(place == iota(place.shape, 0)).astype(BF16)
    high, low = split(taps)
    return dot(high, pick, 1, 0) + dot(low, pick, 1, 0)


def valid_rows(rows):
    q = iota((rows, stack_base(rows)), 1)
    gap = q % rows - iota((rows, stack_base(rows)), 0)
    return (gap >= -REACH) & (gap <= REACH)


def valid_halo():
    r = iota((8, 128), 0)
    q = iota((8, 128), 1)
    t = q % HALO
    inside = q < KS * HALO
    low = (r < REACH) & (t >= REACH) & (t < 2 * REACH) & inside
    up = (r >= 8 - REACH) & (t < REACH) & inside
    return low, up


def tap_matrix(row, rows):
    base = stack_base(rows)
    parts = [
        pltpu.roll(jnp.broadcast_to(row[:, v : v + 128], (rows, 128)), 0, 1, stride=1, stride_axis=0)
        for v in range(0, base, 128)
    ]
    own = jnp.where(valid_rows(rows), jnp.concatenate(parts, axis=1), 0.0)
    low_ok, up_ok = valid_halo()
    low = jnp.broadcast_to(row[:, base : base + 128], (8, 128))
    up = jnp.broadcast_to(row[:, base + 128 :], (8, 128))
    low = jnp.where(low_ok, pltpu.roll(low, 0, 1, stride=1, stride_axis=0), 0.0)
    up = jnp.where(up_ok, pltpu.roll(up, 128 - 7, 1, stride=1, stride_axis=0), 0.0)
    halo = jnp.concatenate([low, jnp.zeros((rows - 16, 128), F32), up], axis=0)
    return jnp.concatenate([own, halo], axis=1)


def tap_sums(m, rows):
    base = stack_base(rows)

    def aligned(v, shift):
        v = pltpu.roll(v, shift % 128, 1, stride=1, stride_axis=0)
        return jnp.sum(v, axis=0, keepdims=True)

    q = iota((rows, base), 1)
    gap = q % rows + iota((rows, base), 0) - (rows - 1)
    own = jnp.where((gap >= -REACH) & (gap <= REACH), m[:, :base], 0.0)
    parts = [aligned(own[:, v : v + 128], 1 - rows) for v in range(0, base, 128)]
    r = iota((8, 128), 0)
    q = iota((8, 128), 1)
    t = q % HALO
    inside = q < KS * HALO
    low_ok = (r >= 8 - REACH) & (t >= REACH) & (t < 2 * REACH) & inside
    up_ok = (r < REACH) & (t < REACH) & inside
    low = jnp.where(low_ok, m[rows - 8 :, base:], 0.0)
    up = jnp.where(up_ok, m[:8, base:], 0.0)
    return jnp.concatenate(parts + [aligned(low, -7), aligned(up, 0)], axis=1)


def shift_stack(own, edge):
    lanes = own.shape[1]
    rows = own.shape[0] - HALO
    lane = iota(own.shape, 1)
    mains, halos = [], []
    for j in range(KS):
        d = j - REACH
        if d == 0:
            s = own
        elif d > 0:
            s = pltpu.roll(jnp.where(lane < d, edge, own), lanes - d, 1)
        else:
            s = pltpu.roll(jnp.where(lane >= lanes + d, edge, own), -d, 1)
        mains.append(s[:rows].astype(BF16))
        halos.append(s[rows:])
    halos.append(jnp.zeros_like(halos[0]))
    pairs = [
        jnp.concatenate([halos[i], halos[i + 1]], axis=0).astype(BF16)
        for i in range(0, KS + 1, 2)
    ]
    gap = jnp.zeros((rows, lanes), BF16)
    rest = jnp.zeros((128 - (KS + 1) * HALO, lanes), BF16)
    return jnp.concatenate(mains + [gap] + pairs + [rest], axis=0)


def stage_halo(north, lat_ref, fold_ref, rb, rh):
    channels, lanes = lat_ref.shape[1], lat_ref.shape[2] // 2
    is_north = north != 0
    for t in range(REACH):
        near = lat_ref[t].astype(F32)
        far = fold_ref[t].astype(F32)
        up = jnp.where(is_north, far, near)
        low = jnp.where(is_north, near, jnp.zeros_like(near))
        rb[pl.ds(t * channels, channels), :] = up[:, :lanes]
        rh[pl.ds(t * channels, channels), :] = up[:, lanes:]
        rb[pl.ds((REACH + t) * channels, channels), :] = low[:, :lanes]
        rh[pl.ds((REACH + t) * channels, channels), :] = low[:, lanes:]
    for t in range(2 * REACH, HALO):
        rb[pl.ds(t * channels, channels), :] = jnp.zeros((channels, lanes), F32)
        rh[pl.ds(t * channels, channels), :] = jnp.zeros((channels, lanes), F32)


def channel_stack(c, first, x_ref, h_ref, rb, rh):
    at = pl.ds(first + c, HALO, stride=rb.shape[0] // HALO)
    own = jnp.concatenate([x_ref[c].astype(F32), rb[at, :]], axis=0)
    edge = jnp.concatenate([h_ref[c].astype(F32), rh[at, :]], axis=0)
    return shift_stack(own, edge)


def lane_edges(cells):
    lanes = cells.shape[1]
    k = iota((2 * HALO, lanes), 0)
    lane = iota((2 * HALO, lanes), 1)
    pick = ((k < REACH) & (lane == k)) | (
        (k >= HALO) & (k < HALO + REACH) & (lane == lanes - REACH + k - HALO)
    )
    return dot(as_f32(pick).astype(BF16), cells, 1, 1)


def pack_kernel(x_ref, lo_ref, hi_ref):
    edges = lane_edges(x_ref[...])
    lo_ref[...] = edges[:HALO].astype(BF16)
    hi_ref[...] = edges[HALO:].astype(BF16)


def unpack_kernel(north_ref, x_ref, east_ref, west_ref, h_ref, lat_ref, fold_ref, xs, hs):
    channels, rows, lanes = x_ref.shape
    k = iota((HALO, lanes), 0)
    lane = iota((HALO, lanes), 1)
    sel_e = as_f32((k < REACH) & (lane == k)).astype(BF16)
    sel_w = as_f32((k < REACH) & (lane == lanes - REACH + k)).astype(BF16)
    sel = jnp.concatenate([sel_e, sel_w], axis=0)
    ed = jnp.concatenate([east_ref[...], west_ref[...]], axis=0)
    hf = dot(ed, sel, 0, 0).reshape(channels, rows, lanes)
    h_ref[...] = hf.astype(BF16)
    g = HALO
    xs[0] = x_ref[:, :16, :].astype(F32)[:, :g].reshape(channels * g, lanes)
    xs[1] = x_ref[:, rows - 16 :, :].astype(F32)[:, 16 - g :].reshape(channels * g, lanes)
    hs[0] = hf[:, :g].reshape(channels * g, lanes)
    hs[1] = hf[:, rows - g :].reshape(channels * g, lanes)
    is_north = north_ref[0] != 0
    rev = as_f32(iota((lanes, lanes), 0) + iota((lanes, lanes), 1) == lanes - 1).astype(BF16)
    for t in range(REACH):
        for part, ref in ((0, xs), (1, hs)):
            bottom = ref.at[0][pl.ds(t, channels, stride=g), :]
            top = ref.at[1][pl.ds(g - REACH + t, channels, stride=g), :]
            span = slice(part * lanes, (part + 1) * lanes)
            lat_ref[t, :, span] = jnp.where(is_north, bottom, top).astype(BF16)
            fold_ref[REACH - 1 - t, :, span] = dot(top.astype(BF16), rev, 1, 0).astype(BF16)


def gelu_parts(hidden):
    k0 = 0.7978845608028654
    k1 = 0.044715 * k0
    sq = hidden * hidden
    th = jnp.tanh(hidden * (k0 + k1 * sq))
    half = 0.5 * th + 0.5
    act = hidden * half
    slope = half + act * (1.0 - th) * (k0 + 3.0 * k1 * sq)
    return act, slope


def main_kernel(
    north_ref, gain_ref, scale_ref, x_ref, h_ref, lat_ref, fold_ref, taps_ref, cot_ref, mask_ref,
    wet_ref, we_ref, wr_ref, wrt_ref,
    out_ref, g_ref, back_ref, low_ref, high_ref, keep_ref, send_ref, sums_ref,
    conv, cots, gs, gr, ms, rb, rh, act_s, hg_s, exp_ref, red_ref, rows_s, gain_s, scale_s,
):
    chunk, rows, lanes = x_ref.shape
    hiddens, channels = wet_ref.shape
    step = pl.program_id(0)

    @pl.when(step == 0)
    def _():
        stage_halo(north_ref[0], lat_ref, fold_ref, rb, rh)
        rows_s[...] = tap_rows(taps_ref[...], rows)

    @pl.when(step < CHUNKS)
    def _():
        first = step * chunk

        def conv_step(k, carry):
            c = first + k
            stack = channel_stack(k, first, x_ref, h_ref, rb, rh)
            high, low = split(tap_matrix(rows_s[pl.ds(c, 1), :], rows))
            both = dot(jnp.concatenate([high, low], axis=0), stack, 1, 0)
            conv[pl.ds(c, rows, stride=channels), :] = both[:rows] + both[rows:]
            wet = mask_ref[...].astype(F32)
            cots[pl.ds(c, rows, stride=channels), :] = cot_ref[k].astype(F32) * wet
            gain_s[pl.ds(c, 1), :] = jnp.full((1, lanes), gain_ref[c])
            scale_s[pl.ds(c, 1), :] = jnp.full((1, lanes), scale_ref[c])
            return carry

        lax.fori_loop(0, chunk, conv_step, 0, unroll=20)

    @pl.when(step == CHUNKS)
    def _():
        cell_work(
            north_ref, wet_ref, we_ref, wr_ref, wrt_ref, keep_ref, send_ref, sums_ref,
            conv, cots, gs, gr, ms, act_s, hg_s, exp_ref, red_ref, gain_s, scale_s, rows,
        )

    @pl.when(step > CHUNKS)
    def _():
        first = (step - CHUNKS - 1) * chunk

        def out_step(k, carry):
            at = pl.multiple_of((first + k) * rows, rows)
            wet = mask_ref[...].astype(F32)
            out_ref[k] = (x_ref[k].astype(F32) + wet * ms[pl.ds(at, rows), :]).astype(BF16)
            g_ref[k] = gs[pl.ds(at, rows), :].astype(BF16)
            back_ref[k] = gr[pl.ds(at, rows), :].astype(BF16)
            return carry

        lax.fori_loop(0, chunk, out_step, 0, unroll=4)
        edges = lane_edges(g_ref[...].reshape(chunk * rows, lanes))
        low_ref[...] = edges[:HALO].astype(BF16)
        high_ref[...] = edges[HALO:].astype(BF16)


def cell_work(
    north_ref, wet_ref, we_ref, wr_ref, wrt_ref, keep_ref, send_ref, sums_ref,
    conv, cots, gs, gr, ms, act_s, hg_s, exp_ref, red_ref, gain_s, scale_s, rows,
):
    hiddens, channels = wet_ref.shape
    lanes = conv.shape[1]
    exp_ref[...] = jnp.zeros_like(exp_ref)
    red_ref[...] = jnp.zeros_like(red_ref)
    sums_ref[...] = jnp.zeros_like(sums_ref)

    def pair(ref, i):
        first = pl.multiple_of(2 * i * channels, 8)
        second = pl.multiple_of((2 * i + 1) * channels, 8)
        return jnp.concatenate(
            [ref[pl.ds(first, channels), :], ref[pl.ds(second, channels), :]], axis=1
        )

    def unpair(ref, i, value):
        ref[pl.ds(2 * i, channels, stride=rows), :] = value[:, :lanes]
        ref[pl.ds(2 * i + 1, channels, stride=rows), :] = value[:, lanes:]

    def cell_step(i, carry):
        gain = jnp.concatenate([gain_s[...]] * 2, axis=1)
        scale = jnp.concatenate([scale_s[...]] * 2, axis=1)
        value = pair(conv, i)
        centred = value - jnp.mean(value, axis=0, keepdims=True)
        inverse = lax.rsqrt(jnp.mean(centred * centred, axis=0, keepdims=True) + 1e-06)
        normalized = centred * inverse
        normed = (normalized * gain).astype(BF16)
        branch = pair(cots, i)
        mixed_grad = (scale * branch).astype(BF16)
        part = 160
        for f in range(0, hiddens, part):
            hidden = dot(wet_ref[f : f + part, :], normed, 1, 0)
            act_grad = dot(wr_ref[f : f + part, :], mixed_grad, 1, 0)
            act, slope = gelu_parts(hidden)
            act_s[f : f + part, :] = act.astype(BF16)
            hg_s[f : f + part, :] = (act_grad * slope).astype(BF16)
        mixed = dot(wrt_ref[...], act_s[...], 1, 0)
        red_ref[...] += dot(act_s[...], mixed_grad, 1, 1)
        normed_grad = dot(we_ref[...], hg_s[...], 1, 0)
        exp_ref[...] += dot(hg_s[...], normed, 1, 1)
        unpair(ms, i, scale * mixed)
        scaled = branch * mixed
        sums_ref[1] += scaled[:, :lanes] + scaled[:, lanes:]
        gained = normed_grad * normalized
        sums_ref[0] += gained[:, :lanes] + gained[:, lanes:]
        unit = normed_grad * gain
        m1 = jnp.mean(unit, axis=0, keepdims=True)
        m2 = jnp.mean(unit * normalized, axis=0, keepdims=True)
        grad = inverse * (unit - m1 - normalized * m2)
        unpair(gs, i, grad)
        gr[pl.ds(rows - 1 - 2 * i, channels, stride=rows), :] = grad[:, :lanes]
        gr[pl.ds(rows - 2 - 2 * i, channels, stride=rows), :] = grad[:, lanes:]
        return carry

    lax.fori_loop(0, rows // 2, cell_step, 0)

    is_north = north_ref[0] != 0
    expand, reduce = exp_ref[...], red_ref[...]
    blank = jnp.zeros((hiddens, 2 * lanes - channels), F32)
    keep_ref[...] = jnp.concatenate([jnp.where(is_north, reduce, expand), blank], axis=1)
    send = jnp.concatenate([jnp.where(is_north, expand, reduce), blank], axis=1)
    send_ref[...] = send.astype(BF16)


def tap_kernel(start, north_ref, x_ref, h_ref, lat_ref, fold_ref, back_ref, sums_ref, small_ref, rb, rh, rows_s):
    chunk, rows, lanes = x_ref.shape
    first = (pl.program_id(0) + start) * chunk

    @pl.when(pl.program_id(0) == 0)
    def _():
        stage_halo(north_ref[0], lat_ref, fold_ref, rb, rh)

    def step(k, carry):
        stack = channel_stack(k, first, x_ref, h_ref, rb, rh)
        rows_s[pl.ds(k, 1), :] = tap_sums(dot(back_ref[k], stack, 1, 1), rows)
        return carry

    lax.fori_loop(0, chunk, step, 0, unroll=20)
    place, _ = tap_places(rows)
    pick = as_f32(place == iota(place.shape, 0))
    pick = jnp.concatenate([pick, jnp.zeros((lanes - KS * KS, pick.shape[1]), F32)], axis=0)
    pick = pick.astype(BF16)
    high, low = split(rows_s[...])
    lane = iota((chunk, lanes), 1)
    small = dot(high, pick, 1, 1) + dot(low, pick, 1, 1)
    for i in range(2):
        total = jnp.sum(sums_ref[i], axis=1, keepdims=True)
        small = jnp.where(lane == KS * KS + i, total, small)
    small_ref[...] = small


def adjoint_kernel(start, north_ref, g_ref, h_ref, lat_ref, fold_ref, taps_ref, cot_ref, *refs):
    out_ref, rb, rh, rows_s = refs[-4:]
    chunk, rows, lanes = g_ref.shape
    first = (pl.program_id(0) + start) * chunk

    @pl.when(pl.program_id(0) == 0)
    def _():
        stage_halo(north_ref[0], lat_ref, fold_ref, rb, rh)
        rows_s[...] = tap_rows(taps_ref[...], rows, north_ref[0])

    def step(k, carry):
        stack = channel_stack(k, first, g_ref, h_ref, rb, rh)
        matrix = tap_matrix(rows_s[pl.ds(first + k, 1), :], rows).astype(BF16)
        out_ref[k] = (cot_ref[k].astype(F32) + dot(matrix, stack, 1, 0)).astype(BF16)
        return carry

    lax.fori_loop(0, chunk, step, 0, unroll=20)


def lon_edges(low, high):
    n = lax.axis_size("lon")
    east = lax.ppermute(low, "lon", [((i + 1) % n, i) for i in range(n)])
    west = lax.ppermute(high, "lon", [(i, (i + 1) % n) for i in range(n)])
    return east, west


def halo_rows(field, east, west, north):
    channels, rows, lanes = field.shape
    n, m = lax.axis_size("lon"), lax.axis_size("lat")
    msg = shape((REACH, channels, 2 * lanes), BF16)
    lane_halo, lat_msg, fold_msg = call(
        unpack_kernel,
        (shape(field.shape, BF16), msg, msg),
        scratch=[pltpu.VMEM((2, channels * HALO, lanes), F32)] * 2,
        n_smem=1,
        n_in=4,
        cost=cost(3),
    )(north, field, east, west)
    fold_rows = lax.ppermute(
        fold_msg, ("lon", "lat"), [(i * m + m - 1, (n - 1 - i) * m + m - 1) for i in range(n)]
    )
    lat_rows = lax.ppermute(lat_msg, "lat", [(0, 1), (1, 0)])
    return lane_halo, lat_rows, fold_rows


def cost(micros):
    return pl.CostEstimate(flops=int(micros * 1e9), bytes_accessed=int(micros * 3e6), transcendentals=0)


def split_half(buf, bit):
    rows, lanes = buf.shape
    if (rows // 2) % 8 and lanes > 128:
        first, second = buf[:, : lanes // 2], buf[:, lanes // 2 :]
    else:
        first, second = buf[: rows // 2], buf[rows // 2 :]
    up = bit != 0
    return jnp.where(up, second, first), jnp.where(up, first, second)


def join_half(mine, other, bit, dims):
    up = bit != 0
    first, second = jnp.where(up, other, mine), jnp.where(up, mine, other)
    return jnp.concatenate([first, second], axis=1 if mine.shape[0] == dims[0] else 0)


def partner(value, axis, b):
    return lax.ppermute(value, axis, [(i, i ^ (1 << b)) for i in range(lax.axis_size(axis))])


def lon_bits():
    return range(lax.axis_size("lon").bit_length() - 1)


def both_sum(value, axis, b):
    mine = value.astype(BF16)
    return mine.astype(F32) + partner(mine, axis, b).astype(F32)


def together(*values):
    return lax.optimization_barrier(values)


def on_device(
    ocean_state, cotangent, kernel, norm_gain, expand_weight, reduce_weight, layer_scale, land_mask
):
    channels, rows, lanes = ocean_state.shape
    hiddens = expand_weight.shape[1]
    width = stack_base(rows) + 256
    is_north = lax.axis_index("lat") == lax.axis_size("lat") - 1
    north = is_north.astype(jnp.int32).reshape(1)
    edge = shape((HALO, channels * rows), BF16)
    field = shape(ocean_state.shape, BF16)
    rowbuf = pltpu.VMEM((HALO * channels, lanes), F32)
    cellbuf = pltpu.VMEM((channels * rows, lanes), F32)
    tapbuf = pltpu.VMEM((channels, width), F32)
    hidbuf = pltpu.VMEM((hiddens, 2 * lanes), BF16)
    gradbuf = pltpu.VMEM((hiddens, channels), F32)
    lanebuf = pltpu.VMEM((channels, lanes), F32)

    low, high = call(pack_kernel, (edge, edge), n_in=1, cost=cost(2))(
        ocean_state.reshape(channels * rows, lanes)
    )
    east, west = lon_edges(low, high)
    halo, lat_rows, fold_rows = halo_rows(ocean_state, east, west, north)

    chunk = channels // CHUNKS
    whole = vmem()

    def block(index):
        return pl.BlockSpec((chunk, rows, lanes), lambda i: (index(i), 0, 0))

    def into(i):
        return jnp.minimum(i, CHUNKS - 1)

    def back_out(i):
        return jnp.maximum(i - CHUNKS - 1, 0)

    def both_ways(i):
        return jnp.where(i <= CHUNKS, into(i), back_out(i))

    edge_block = pl.BlockSpec((HALO, chunk * rows), lambda i: (0, back_out(i)))
    block_out, conv_grad, back_grad, g_low, g_high, keep, send, sums = grid_call(
        main_kernel,
        2 * CHUNKS + 1,
        (
            field,
            field,
            field,
            edge,
            edge,
            shape((hiddens, 2 * lanes), F32),
            shape((hiddens, 2 * lanes), BF16),
            shape((2, channels, lanes), F32),
        ),
        [smem()] * 3 + [block(both_ways), block(into), whole, whole, whole, block(into)] + [whole] * 5,
        [block(back_out)] * 3 + [edge_block] * 2 + [whole] * 3,
        [cellbuf] * 5 + [rowbuf] * 2 + [hidbuf] * 2 + [gradbuf] * 2 + [tapbuf] + [lanebuf] * 2,
        cost(40),
    )(
        north, norm_gain, layer_scale, ocean_state, halo, lat_rows, fold_rows, kernel, cotangent,
        land_mask, expand_weight.T, expand_weight, reduce_weight, reduce_weight.T,
    )

    def taps_part(start, count, field, back):
        here = block(lambda i: i + start)
        return grid_call(
            functools.partial(tap_kernel, start),
            count,
            shape((count * chunk, lanes), F32),
            [smem(), here, here, whole, whole, here]
            + [pl.BlockSpec((2, chunk, lanes), lambda i: (0, i + start, 0))],
            pl.BlockSpec((chunk, lanes), lambda i: (i, 0)),
            [rowbuf] * 2 + [pltpu.VMEM((chunk, width), F32)],
            cost(3 * count),
        )(north, field, halo, lat_rows, fold_rows, back, sums)

    def adjoint_part(start, count, grad, lane_halo, previous):
        here = block(lambda i: i + start)
        extra = () if previous is None else (previous,)
        return grid_call(
            functools.partial(adjoint_kernel, start),
            count,
            shape(ocean_state.shape, BF16),
            [smem(), here, here, whole, whole, whole, here]
            + [pl.BlockSpec(memory_space=pl.ANY)] * len(extra),
            here,
            [rowbuf] * 2 + [tapbuf],
            cost(2 * count),
            {7: 0} if extra else None,
        )(north, grad, lane_halo, g_lat, g_fold, kernel, cotangent, *extra)

    bits = list(lon_bits())
    first_part = (CHUNKS + 1) // 2

    def side(b):
        return (lax.axis_index("lon") >> b) & 1

    g_east, g_west = lon_edges(g_low, g_high)
    buf = keep + partner(send, "lat", 0).astype(F32)
    sizes, parts = [], []
    back = back_grad
    for b in bits:
        sizes.append(buf.shape)
        stay, go = split_half(buf, side(b))
        got = partner(go.astype(BF16), "lon", b)
        if len(parts) < 2:
            start = len(parts) * first_part
            count = CHUNKS - first_part if parts else first_part
            parts.append(taps_part(start, count, ocean_state, back))
            got, back = together(got, parts[-1], back)[::2]
        buf = stay + got.astype(F32)
    small = jnp.concatenate(parts, axis=0)
    g_halo, g_lat, g_fold = halo_rows(conv_grad, g_east, g_west, north)
    buf = buf.astype(BF16)
    state_grad = None
    done = 0
    grad = conv_grad
    for n, b in enumerate(bits[::-1]):
        got = partner(buf, "lon", b)
        small = both_sum(small, "lon", b)
        if n > 0 and done < CHUNKS:
            count = min(2, CHUNKS - done)
            state_grad = adjoint_part(done, count, grad, g_halo, state_grad)
            done += count
            got, state_grad, grad = together(got, state_grad, grad)
        buf = join_half(buf, got, side(b), sizes[len(bits) - 1 - n])
    if done < CHUNKS:
        state_grad = adjoint_part(done, CHUNKS - done, grad, g_halo, state_grad)
    other = partner(buf, "lat", 0)
    small = both_sum(small, "lat", 0)
    expand = jnp.where(is_north, other, buf)[:, :channels].astype(F32)
    reduce = jnp.where(is_north, buf, other)[:, :channels].astype(F32)
    kernel_grad = small[:, : KS * KS]
    gain_grad = small[:, KS * KS]
    scale_grad = small[:, KS * KS + 1]
    return (block_out, state_grad, kernel_grad, gain_grad, expand.T, reduce, scale_grad)


def solution(mesh):
    tiles = P(None, ("members", "lat"), "lon")
    return jax.shard_map(
        on_device,
        mesh=mesh,
        in_specs=(tiles, tiles, P(), P(), P(), P(), P(), P("lat", "lon")),
        out_specs=(
            tiles, tiles, P("members", None), P("members"), P("members", None),
            P("members", None), P("members"),
        ),
        check_vma=False,
    )
```

```python
import functools

import jax
import jax.numpy as jnp
from jax import lax
from jax.experimental import pallas as pl
from jax.experimental.pallas import tpu as pltpu
from jax.sharding import PartitionSpec as P

KS = 7
REACH = KS // 2
F32 = jnp.float32
BF16 = jnp.bfloat16
HALO = 8
VMEM_LIMIT = 58 << 20
CHUNKS = 5
WIDE = 8
SMALL = 64
PITCH = 40


def vmem():
    return pl.BlockSpec(memory_space=pltpu.VMEM)


def smem():
    return pl.BlockSpec(memory_space=pltpu.SMEM)


def call(body, outs, scratch=(), n_smem=0, n_in=0, cost=None):
    return pl.pallas_call(
        body,
        out_shape=outs,
        in_specs=[smem()] * n_smem + [vmem()] * (n_in - n_smem),
        out_specs=jax.tree.map(lambda _: vmem(), outs),
        scratch_shapes=list(scratch),
        compiler_params=pltpu.CompilerParams(vmem_limit_bytes=VMEM_LIMIT),
        cost_estimate=cost,
    )


def grid_call(body, grid, outs, in_specs, out_specs, scratch, cost, aliases=None):
    return pl.pallas_call(
        body,
        grid=(grid,),
        out_shape=outs,
        in_specs=in_specs,
        out_specs=out_specs,
        scratch_shapes=list(scratch),
        input_output_aliases=aliases or {},
        compiler_params=pltpu.CompilerParams(
            vmem_limit_bytes=VMEM_LIMIT, dimension_semantics=("arbitrary",)
        ),
        cost_estimate=cost,
    )


def dot(a, b, ca, cb):
    return lax.dot_general(a, b, (((ca,), (cb,)), ((), ())), preferred_element_type=F32)


def shape(dims, dtype):
    return jax.ShapeDtypeStruct(dims, dtype)


def iota(dims, axis):
    return lax.broadcasted_iota(jnp.int32, dims, axis)


def as_f32(mask):
    return jnp.where(mask, 1.0, 0.0).astype(F32)


def stack_base(rows):
    return (KS + 1) * rows


def tap_places(rows):
    width = stack_base(rows) + 256
    q = iota((KS * KS, width), 1)
    base = stack_base(rows)
    w = q % 128 + REACH
    w = jnp.where(w >= 128, w - 128, w)
    row_j = q // 128 * (128 // rows) + w // rows
    row_a = w % rows
    t = q % HALO
    halo_j = (q - base) % 128 // HALO
    upper = q >= base + 128
    halo_a = jnp.where(upper, t + REACH + 1, t - REACH)
    j = jnp.where(q < base, row_j, halo_j)
    a = jnp.where(q < base, row_a, halo_a)
    halo_ok = (upper & (t < REACH)) | ((q < base + 128) & (t >= REACH) & (t < 2 * REACH))
    ok = (j < KS) & (a < KS) & (a >= 0) & ((q < base) | halo_ok)
    return jnp.where(ok, a * KS + j, -1), upper


def split(value):
    high = value.astype(BF16)
    return high, (value - high.astype(F32)).astype(BF16)


def tap_rows(taps, rows, adjoint=None):
    place, upper = tap_places(rows)
    if adjoint is not None:
        keep = (upper & (adjoint != 0)) | (place < 0)
        place = jnp.where(keep, place, KS * KS - 1 - place)
    pick = as_f32(place == iota(place.shape, 0)).astype(BF16)
    high, low = split(taps)
    return dot(high, pick, 1, 0) + dot(low, pick, 1, 0)


def valid_rows(rows):
    q = iota((rows, stack_base(rows)), 1)
    gap = q % rows - iota((rows, stack_base(rows)), 0)
    return (gap >= -REACH) & (gap <= REACH)


def valid_halo():
    r = iota((8, 128), 0)
    q = iota((8, 128), 1)
    t = q % HALO
    inside = q < KS * HALO
    low = (r < REACH) & (t >= REACH) & (t < 2 * REACH) & inside
    up = (r >= 8 - REACH) & (t < REACH) & inside
    return low, up


def tap_matrix(row, rows):
    base = stack_base(rows)
    parts = [
        pltpu.roll(jnp.broadcast_to(row[:, v : v + 128], (rows, 128)), 0, 1, stride=1, stride_axis=0)
        for v in range(0, base, 128)
    ]
    own = jnp.where(valid_rows(rows), jnp.concatenate(parts, axis=1), 0.0)
    low_ok, up_ok = valid_halo()
    low = jnp.broadcast_to(row[:, base : base + 128], (8, 128))
    up = jnp.broadcast_to(row[:, base + 128 :], (8, 128))
    low = jnp.where(low_ok, pltpu.roll(low, 0, 1, stride=1, stride_axis=0), 0.0)
    up = jnp.where(up_ok, pltpu.roll(up, 128 - 7, 1, stride=1, stride_axis=0), 0.0)
    halo = jnp.concatenate([low, jnp.zeros((rows - 16, 128), F32), up], axis=0)
    return jnp.concatenate([own, halo], axis=1)


def tap_sums(m, rows):
    base = stack_base(rows)

    def aligned(v, shift):
        v = pltpu.roll(v, shift % 128, 1, stride=1, stride_axis=0)
        return jnp.sum(v, axis=0, keepdims=True)

    q = iota((rows, base), 1)
    gap = q % rows + iota((rows, base), 0) - (rows - 1)
    own = jnp.where((gap >= -REACH) & (gap <= REACH), m[:, :base], 0.0)
    parts = [aligned(own[:, v : v + 128], 1 - rows) for v in range(0, base, 128)]
    r = iota((8, 128), 0)
    q = iota((8, 128), 1)
    t = q % HALO
    inside = q < KS * HALO
    low_ok = (r >= 8 - REACH) & (t >= REACH) & (t < 2 * REACH) & inside
    up_ok = (r < REACH) & (t < REACH) & inside
    low = jnp.where(low_ok, m[rows - 8 :, base:], 0.0)
    up = jnp.where(up_ok, m[:8, base:], 0.0)
    return jnp.concatenate(parts + [aligned(low, -7), aligned(up, 0)], axis=1)


def shift_stack(own, edge):
    lanes = own.shape[1]
    rows = own.shape[0] - HALO
    lane = iota(own.shape, 1)
    mains, halos = [], []
    for j in range(KS):
        d = j - REACH
        if d == 0:
            s = own
        elif d > 0:
            s = pltpu.roll(jnp.where(lane < d, edge, own), lanes - d, 1)
        else:
            s = pltpu.roll(jnp.where(lane >= lanes + d, edge, own), -d, 1)
        mains.append(s[:rows].astype(BF16))
        halos.append(s[rows:])
    halos.append(jnp.zeros_like(halos[0]))
    pairs = [
        jnp.concatenate([halos[i], halos[i + 1]], axis=0).astype(BF16)
        for i in range(0, KS + 1, 2)
    ]
    gap = jnp.zeros((rows, lanes), BF16)
    rest = jnp.zeros((128 - (KS + 1) * HALO, lanes), BF16)
    return jnp.concatenate(mains + [gap] + pairs + [rest], axis=0)


def stage_halo(north, lat_ref, fold_ref, rb, rh):
    channels, lanes = lat_ref.shape[1], lat_ref.shape[2] // 2
    is_north = north != 0
    for t in range(REACH):
        near = lat_ref[t].astype(F32)
        far = fold_ref[t].astype(F32)
        up = jnp.where(is_north, far, near)
        low = jnp.where(is_north, near, jnp.zeros_like(near))
        rb[pl.ds(t * channels, channels), :] = up[:, :lanes]
        rh[pl.ds(t * channels, channels), :] = up[:, lanes:]
        rb[pl.ds((REACH + t) * channels, channels), :] = low[:, :lanes]
        rh[pl.ds((REACH + t) * channels, channels), :] = low[:, lanes:]
    for t in range(2 * REACH, HALO):
        rb[pl.ds(t * channels, channels), :] = jnp.zeros((channels, lanes), F32)
        rh[pl.ds(t * channels, channels), :] = jnp.zeros((channels, lanes), F32)


def channel_stack(c, first, x_ref, h_ref, rb, rh):
    at = pl.ds(first + c, HALO, stride=rb.shape[0] // HALO)
    own = jnp.concatenate([x_ref[c].astype(F32), rb[at, :]], axis=0)
    edge = jnp.concatenate([h_ref[c].astype(F32), rh[at, :]], axis=0)
    return shift_stack(own, edge)


def lane_edges(cells):
    lanes = cells.shape[1]
    k = iota((2 * HALO, lanes), 0)
    lane = iota((2 * HALO, lanes), 1)
    pick = ((k < REACH) & (lane == k)) | (
        (k >= HALO) & (k < HALO + REACH) & (lane == lanes - REACH + k - HALO)
    )
    return dot(as_f32(pick).astype(BF16), cells, 1, 1)


def pack_kernel(x_ref, lo_ref, hi_ref):
    edges = lane_edges(x_ref[...])
    lo_ref[...] = edges[:HALO].astype(BF16)
    hi_ref[...] = edges[HALO:].astype(BF16)


def unpack_kernel(north_ref, x_ref, east_ref, west_ref, h_ref, lat_ref, fold_ref, xs, hs):
    channels, rows, lanes = x_ref.shape
    k = iota((HALO, lanes), 0)
    lane = iota((HALO, lanes), 1)
    sel_e = as_f32((k < REACH) & (lane == k)).astype(BF16)
    sel_w = as_f32((k < REACH) & (lane == lanes - REACH + k)).astype(BF16)
    sel = jnp.concatenate([sel_e, sel_w], axis=0)
    ed = jnp.concatenate([east_ref[...], west_ref[...]], axis=0)
    hf = dot(ed, sel, 0, 0).reshape(channels, rows, lanes)
    h_ref[...] = hf.astype(BF16)
    g = HALO
    xs[0] = x_ref[:, :16, :].astype(F32)[:, :g].reshape(channels * g, lanes)
    xs[1] = x_ref[:, rows - 16 :, :].astype(F32)[:, 16 - g :].reshape(channels * g, lanes)
    hs[0] = hf[:, :g].reshape(channels * g, lanes)
    hs[1] = hf[:, rows - g :].reshape(channels * g, lanes)
    is_north = north_ref[0] != 0
    rev = as_f32(iota((lanes, lanes), 0) + iota((lanes, lanes), 1) == lanes - 1).astype(BF16)
    for t in range(REACH):
        for part, ref in ((0, xs), (1, hs)):
            bottom = ref.at[0][pl.ds(t, channels, stride=g), :]
            top = ref.at[1][pl.ds(g - REACH + t, channels, stride=g), :]
            span = slice(part * lanes, (part + 1) * lanes)
            lat_ref[t, :, span] = jnp.where(is_north, bottom, top).astype(BF16)
            fold_ref[REACH - 1 - t, :, span] = dot(top.astype(BF16), rev, 1, 0).astype(BF16)


def gelu_parts(hidden):
    k0 = 0.7978845608028654
    k1 = 0.044715 * k0
    sq = hidden * hidden
    th = jnp.tanh(hidden * (k0 + k1 * sq))
    half = 0.5 * th + 0.5
    act = hidden * half
    slope = half + act * (1.0 - th) * (k0 + 3.0 * k1 * sq)
    return act, slope


def main_kernel(
    north_ref, gain_ref, scale_ref, x_ref, h_ref, lat_ref, fold_ref, taps_ref, cot_ref, mask_ref,
    wet_ref, we_ref, wr_ref, wrt_ref,
    out_ref, g_ref, back_ref, low_ref, high_ref, keep_ref, send_ref, sums_ref,
    conv, cots, gs, gr, ms, rb, rh, act_s, hg_s, exp_ref, red_ref, rows_s, gain_s, scale_s,
):
    chunk, rows, lanes = x_ref.shape
    hiddens, channels = wet_ref.shape
    step = pl.program_id(0)

    @pl.when(step == 0)
    def _():
        stage_halo(north_ref[0], lat_ref, fold_ref, rb, rh)
        rows_s[...] = tap_rows(taps_ref[...], rows)

    @pl.when(step < CHUNKS)
    def _():
        first = step * chunk

        def conv_step(k, carry):
            c = first + k
            stack = channel_stack(k, first, x_ref, h_ref, rb, rh)
            high, low = split(tap_matrix(rows_s[pl.ds(c, 1), :], rows))
            both = dot(jnp.concatenate([high, low], axis=0), stack, 1, 0)
            conv[pl.ds(c, rows, stride=channels), :] = both[:rows] + both[rows:]
            wet = mask_ref[...].astype(F32)
            cots[pl.ds(c, rows, stride=channels), :] = cot_ref[k].astype(F32) * wet
            gain_s[pl.ds(c, 1), :] = jnp.full((1, lanes), gain_ref[c])
            scale_s[pl.ds(c, 1), :] = jnp.full((1, lanes), scale_ref[c])
            return carry

        lax.fori_loop(0, chunk, conv_step, 0, unroll=20)

    @pl.when(step == CHUNKS)
    def _():
        cell_work(
            north_ref, wet_ref, we_ref, wr_ref, wrt_ref, keep_ref, send_ref, sums_ref,
            conv, cots, gs, gr, ms, act_s, hg_s, exp_ref, red_ref, gain_s, scale_s, rows,
        )

    @pl.when(step > CHUNKS)
    def _():
        first = (step - CHUNKS - 1) * chunk

        def out_step(k, carry):
            at = pl.multiple_of((first + k) * PITCH, 8)
            wet = mask_ref[...].astype(F32)
            out_ref[k] = (x_ref[k].astype(F32) + wet * ms[pl.ds(at, rows), :]).astype(BF16)
            g_ref[k] = gs[pl.ds(at, rows), :].astype(BF16)
            back_ref[k] = gr[pl.ds(at, rows), :].astype(BF16)
            return carry

        lax.fori_loop(0, chunk, out_step, 0, unroll=10)
        edges = lane_edges(g_ref[...].reshape(chunk * rows, lanes))
        low_ref[...] = edges[:HALO].astype(BF16)
        high_ref[...] = edges[HALO:].astype(BF16)


def cell_work(
    north_ref, wet_ref, we_ref, wr_ref, wrt_ref, keep_ref, send_ref, sums_ref,
    conv, cots, gs, gr, ms, act_s, hg_s, exp_ref, red_ref, gain_s, scale_s, rows,
):
    hiddens, channels = wet_ref.shape
    lanes = conv.shape[1]
    exp_ref[...] = jnp.zeros_like(exp_ref)
    red_ref[...] = jnp.zeros_like(red_ref)
    sums_ref[...] = jnp.zeros_like(sums_ref)

    def cat(values):
        return jnp.concatenate(values, axis=1)

    def group(ref, i):
        at = [pl.multiple_of((WIDE * i + k) * channels, 8) for k in range(WIDE)]
        return cat([ref[pl.ds(a, channels), :] for a in at])

    def ungroup(ref, i, value):
        for k in range(WIDE):
            ref[pl.ds(WIDE * i + k, channels, stride=PITCH), :] = value[:, k * lanes : (k + 1) * lanes]

    def fold(value):
        return sum(value[:, k * lanes : (k + 1) * lanes] for k in range(WIDE))

    def cell_step(i, carry):
        gain = cat([gain_s[...]] * WIDE)
        scale = cat([scale_s[...]] * WIDE)
        value = group(conv, i)
        centred = value - jnp.mean(value, axis=0, keepdims=True)
        inverse = lax.rsqrt(jnp.mean(centred * centred, axis=0, keepdims=True) + 1e-06)
        normalized = centred * inverse
        normed = (normalized * gain).astype(BF16)
        branch = group(cots, i)
        mixed_grad = (scale * branch).astype(BF16)
        part = 160
        for f in range(0, hiddens, part):
            hidden = dot(wet_ref[f : f + part, :], normed, 1, 0)
            act_grad = dot(wr_ref[f : f + part, :], mixed_grad, 1, 0)
            act, slope = gelu_parts(hidden)
            act_s[f : f + part, :] = act.astype(BF16)
            hg_s[f : f + part, :] = (act_grad * slope).astype(BF16)
        mixed = dot(wrt_ref[...], act_s[...], 1, 0)
        red_ref[...] += dot(act_s[...], mixed_grad, 1, 1)
        normed_grad = dot(we_ref[...], hg_s[...], 1, 0)
        exp_ref[...] += dot(hg_s[...], normed, 1, 1)
        ungroup(ms, i, scale * mixed)
        sums_ref[1] += fold(branch * mixed)
        sums_ref[0] += fold(normed_grad * normalized)
        unit = normed_grad * gain
        m1 = jnp.mean(unit, axis=0, keepdims=True)
        m2 = jnp.mean(unit * normalized, axis=0, keepdims=True)
        grad = inverse * (unit - m1 - normalized * m2)
        ungroup(gs, i, grad)
        for k in range(WIDE):
            at = pl.ds(rows - 1 - WIDE * i - k, channels, stride=PITCH)
            gr[at, :] = grad[:, k * lanes : (k + 1) * lanes]
        return carry

    lax.fori_loop(0, rows // WIDE, cell_step, 0)
    is_north = north_ref[0] != 0
    expand, reduce = exp_ref[...], red_ref[...]
    mine = jnp.where(is_north, reduce, expand)
    theirs = jnp.where(is_north, expand, reduce)
    blank = jnp.zeros((hiddens, 2 * lanes - channels), F32)
    for ref, value in ((keep_ref, mine), (send_ref, theirs)):
        ref[:hiddens, :] = value[:, :lanes].astype(ref.dtype)
        ref[hiddens:, :] = cat([value[:, lanes:], blank]).astype(ref.dtype)


def tap_kernel(start, north_ref, x_ref, h_ref, lat_ref, fold_ref, back_ref, sums_ref, small_ref, rb, rh, rows_s):
    chunk, rows, lanes = x_ref.shape
    first = (pl.program_id(0) + start) * chunk

    @pl.when(pl.program_id(0) == 0)
    def _():
        stage_halo(north_ref[0], lat_ref, fold_ref, rb, rh)

    def step(k, carry):
        stack = channel_stack(k, first, x_ref, h_ref, rb, rh)
        rows_s[pl.ds(k, 1), :] = tap_sums(dot(back_ref[k], stack, 1, 1), rows)
        return carry

    lax.fori_loop(0, chunk, step, 0, unroll=20)
    place, _ = tap_places(rows)
    pick = as_f32(place == iota(place.shape, 0))
    blank = jnp.zeros((SMALL - KS * KS, pick.shape[1]), F32)
    pick = jnp.concatenate([pick, blank], axis=0).astype(BF16)
    high, low = split(rows_s[...])
    taps = dot(high, pick, 1, 1) + dot(low, pick, 1, 1)
    lane = iota((chunk, SMALL), 1)
    for i in range(2):
        total = jnp.sum(sums_ref[i], axis=1, keepdims=True)
        taps = jnp.where(lane == KS * KS + i, total, taps)
    small_ref[...] = taps


def adjoint_kernel(start, north_ref, g_ref, h_ref, lat_ref, fold_ref, taps_ref, cot_ref, *refs):
    out_ref, rb, rh, rows_s = refs[-4:]
    chunk, rows, lanes = g_ref.shape
    first = (pl.program_id(0) + start) * chunk

    @pl.when(pl.program_id(0) == 0)
    def _():
        stage_halo(north_ref[0], lat_ref, fold_ref, rb, rh)
        rows_s[...] = tap_rows(taps_ref[...], rows, north_ref[0])

    def step(k, carry):
        stack = channel_stack(k, first, g_ref, h_ref, rb, rh)
        matrix = tap_matrix(rows_s[pl.ds(first + k, 1), :], rows).astype(BF16)
        out_ref[k] = (cot_ref[k].astype(F32) + dot(matrix, stack, 1, 0)).astype(BF16)
        return carry

    lax.fori_loop(0, chunk, step, 0, unroll=20)


def lon_edges(low, high):
    n = lax.axis_size("lon")
    east = lax.ppermute(low, "lon", [((i + 1) % n, i) for i in range(n)])
    west = lax.ppermute(high, "lon", [(i, (i + 1) % n) for i in range(n)])
    return east, west


def halo_rows(field, east, west, north):
    channels, rows, lanes = field.shape
    n, m = lax.axis_size("lon"), lax.axis_size("lat")
    msg = shape((REACH, channels, 2 * lanes), BF16)
    lane_halo, lat_msg, fold_msg = call(
        unpack_kernel,
        (shape(field.shape, BF16), msg, msg),
        scratch=[pltpu.VMEM((2, channels * HALO, lanes), F32)] * 2,
        n_smem=1,
        n_in=4,
        cost=cost(3),
    )(north, field, east, west)
    fold_rows = lax.ppermute(
        fold_msg, ("lon", "lat"), [(i * m + m - 1, (n - 1 - i) * m + m - 1) for i in range(n)]
    )
    lat_rows = lax.ppermute(lat_msg, "lat", [(0, 1), (1, 0)])
    return lane_halo, lat_rows, fold_rows


def cost(micros):
    return pl.CostEstimate(flops=int(micros * 1e9), bytes_accessed=int(micros * 3e6), transcendentals=0)


def halves(buf, bit):
    half = buf.shape[0] // 2
    first, second = buf[:half], buf[half:]
    up = bit != 0
    return jnp.where(up, second, first), jnp.where(up, first, second)


def joined(mine, other, bit):
    up = bit != 0
    return jnp.concatenate([jnp.where(up, other, mine), jnp.where(up, mine, other)], axis=0)


def partner(value, axis, b):
    return lax.ppermute(value, axis, [(i, i ^ (1 << b)) for i in range(lax.axis_size(axis))])


def lon_bits():
    return range(lax.axis_size("lon").bit_length() - 1)


def together(*values):
    return lax.optimization_barrier(values)


def on_device(
    ocean_state, cotangent, kernel, norm_gain, expand_weight, reduce_weight, layer_scale, land_mask
):
    channels, rows, lanes = ocean_state.shape
    hiddens = expand_weight.shape[1]
    width = stack_base(rows) + 256
    is_north = lax.axis_index("lat") == lax.axis_size("lat") - 1
    north = is_north.astype(jnp.int32).reshape(1)
    edge = shape((HALO, channels * rows), BF16)
    field = shape(ocean_state.shape, BF16)
    rowbuf = pltpu.VMEM((HALO * channels, lanes), F32)
    cellbuf = pltpu.VMEM((channels * rows, lanes), F32)
    pitchbuf = pltpu.VMEM((channels * PITCH, lanes), F32)
    tapbuf = pltpu.VMEM((channels, width), F32)
    hidbuf = pltpu.VMEM((hiddens, WIDE * lanes), BF16)
    gradbuf = pltpu.VMEM((hiddens, channels), F32)
    lanebuf = pltpu.VMEM((channels, lanes), F32)

    low, high = call(pack_kernel, (edge, edge), n_in=1, cost=cost(2))(
        ocean_state.reshape(channels * rows, lanes)
    )
    east, west = lon_edges(low, high)
    halo, lat_rows, fold_rows = halo_rows(ocean_state, east, west, north)

    chunk = channels // CHUNKS
    whole = vmem()

    def block(index):
        return pl.BlockSpec((chunk, rows, lanes), lambda i: (index(i), 0, 0))

    def into(i):
        return jnp.minimum(i, CHUNKS - 1)

    def back_out(i):
        return jnp.maximum(i - CHUNKS - 1, 0)

    def both_ways(i):
        return jnp.where(i <= CHUNKS, into(i), back_out(i))

    edge_block = pl.BlockSpec((HALO, chunk * rows), lambda i: (0, back_out(i)))
    block_out, conv_grad, back_grad, g_low, g_high, keep, send, sums = grid_call(
        main_kernel,
        2 * CHUNKS + 1,
        (
            field,
            field,
            field,
            edge,
            edge,
            shape((2 * hiddens, lanes), F32),
            shape((2 * hiddens, lanes), BF16),
            shape((2, channels, lanes), F32),
        ),
        [smem()] * 3 + [block(both_ways), block(into)] + [whole] * 3 + [block(into)] + [whole] * 5,
        [block(back_out)] * 3 + [edge_block] * 2 + [whole] * 3,
        [cellbuf] * 2 + [pitchbuf] * 3 + [rowbuf] * 2 + [hidbuf] * 2 + [gradbuf] * 2 + [tapbuf] + [lanebuf] * 2,
        cost(40),
    )(
        north, norm_gain, layer_scale, ocean_state, halo, lat_rows, fold_rows, kernel, cotangent, land_mask,
         expand_weight.T, expand_weight, reduce_weight, reduce_weight.T,
    )

    def adjoint_part(start, count, grad, lane_halo, previous):
        here = block(lambda i: i + start)
        extra = () if previous is None else (previous,)
        return grid_call(
            functools.partial(adjoint_kernel, start),
            count,
            field,
            [smem(), here, here] + [whole] * 3 + [here]
            + [pl.BlockSpec(memory_space=pl.ANY)] * len(extra),
            here,
            [rowbuf] * 2 + [tapbuf],
            cost(2 * count),
            {7: 0} if extra else None,
        )(north, grad, lane_halo, g_lat, g_fold, kernel, cotangent, *extra)

    g_east, g_west = lon_edges(g_low, g_high)
    def taps_part(start, count, back):
        here = block(lambda i: i + start)
        return grid_call(
            functools.partial(tap_kernel, start),
            count,
            shape((count * chunk, SMALL), F32),
            [smem(), here, here] + [whole] * 2
            + [here, pl.BlockSpec((2, chunk, lanes), lambda i: (0, i + start, 0))],
            pl.BlockSpec((chunk, SMALL), lambda i: (i, 0)),
            [rowbuf] * 2 + [pltpu.VMEM((chunk, width), F32)],
            cost(3 * count),
        )(north, ocean_state, halo, lat_rows, fold_rows, back, sums)

    buf = keep + partner(send, "lat", 0).astype(F32)
    bits = list(lon_bits())
    parts, taps_done, back = [], 0, back_grad
    g_halo, state_grad, done, grad = None, None, 0, conv_grad
    steps = [(b, True) for b in bits] + [(b, False) for b in bits[::-1]]
    for b, halving in steps:
        bit = (lax.axis_index("lon") >> b) & 1
        if halving:
            stay, go = halves(buf, bit)
            go = go.astype(BF16)
        else:
            if done == 0:
                small = jnp.concatenate(parts, axis=0)
                half = channels // 2
                small = jnp.concatenate([small[:half], small[half:]], axis=1)
                small = jnp.pad(small, ((0, -half % 8), (0, 0)))
                small = small + partner(small, "lat", 0)
            stay, own = buf.astype(BF16), small.astype(BF16)
            go = jnp.concatenate([stay, own], axis=0)
        go, grad, back = together(go, grad, back)
        got = partner(go, "lon", b)
        if taps_done and g_halo is None:
            g_halo, g_lat, g_fold = halo_rows(grad, g_east, g_west, north)
            got, g_halo, back = together(got, g_halo, back)
        elif taps_done < CHUNKS:
            count = min(CHUNKS - taps_done, (CHUNKS + 1) // 2)
            parts.append(taps_part(taps_done, count, back))
            taps_done += count
            got, parts[-1] = together(got, parts[-1])
        elif done < CHUNKS and not halving:
            count = min(2, CHUNKS - done)
            state_grad = adjoint_part(done, count, grad, g_halo, state_grad)
            done += count
            got, state_grad = together(got, state_grad)
        if halving:
            buf = stay + got.astype(F32)
        else:
            rows_here = stay.shape[0]
            buf = joined(stay, got[:rows_here], bit)
            small = own.astype(F32) + got[rows_here:].astype(F32)
    if done < CHUNKS:
        state_grad = adjoint_part(done, CHUNKS - done, grad, g_halo, state_grad)
    other = partner(buf, "lat", 0)

    def unfolded(value):
        top, rest = value[:hiddens], value[hiddens:, : channels - lanes]
        return jnp.concatenate([top, rest], axis=1).astype(F32)

    expand = unfolded(jnp.where(is_north, other, buf))
    reduce = unfolded(jnp.where(is_north, buf, other))
    half = channels // 2
    small = jnp.concatenate([small[:half, :SMALL], small[:half, SMALL:]], axis=0)
    kernel_grad = small[:, : KS * KS]
    gain_grad = small[:, KS * KS]
    scale_grad = small[:, KS * KS + 1]
    return (block_out, state_grad, kernel_grad, gain_grad, expand.T, reduce, scale_grad)


def solution(mesh):
    tiles = P(None, ("members", "lat"), "lon")
    return jax.shard_map(
        on_device,
        mesh=mesh,
        in_specs=(tiles, tiles, P(), P(), P(), P(), P(), P("lat", "lon")),
        out_specs=(
            tiles, tiles, P("members", None), P("members"), P("members", None),
            P("members", None), P("members"),
        ),
        check_vma=False,
    )
```

```python
import jax
import jax.numpy as jnp
from jax import lax
from jax.experimental import pallas as pl
from jax.experimental.pallas import tpu as pltpu
from jax.sharding import PartitionSpec as P

KS = 7
REACH = KS // 2
F32 = jnp.float32
BF16 = jnp.bfloat16
HALO = 8
VMEM_LIMIT = 58 << 20
CHUNKS = 5
MAIN = 1
WIDE = 8
SMALL = 64
PITCH = 40


def vmem():
    return pl.BlockSpec(memory_space=pltpu.VMEM)


def smem():
    return pl.BlockSpec(memory_space=pltpu.SMEM)


def call(body, outs, scratch=(), n_smem=0, n_in=0, cost=None):
    return pl.pallas_call(
        body,
        out_shape=outs,
        in_specs=[smem()] * n_smem + [vmem()] * (n_in - n_smem),
        out_specs=jax.tree.map(lambda _: vmem(), outs),
        scratch_shapes=list(scratch),
        compiler_params=pltpu.CompilerParams(vmem_limit_bytes=VMEM_LIMIT),
        cost_estimate=cost,
    )


def grid_call(body, grid, outs, in_specs, out_specs, scratch, cost, aliases=None):
    return pl.pallas_call(
        body,
        grid=(grid,),
        out_shape=outs,
        in_specs=in_specs,
        out_specs=out_specs,
        scratch_shapes=list(scratch),
        input_output_aliases=aliases or {},
        compiler_params=pltpu.CompilerParams(
            vmem_limit_bytes=VMEM_LIMIT, dimension_semantics=("arbitrary",)
        ),
        cost_estimate=cost,
    )


def dot(a, b, ca, cb):
    return lax.dot_general(a, b, (((ca,), (cb,)), ((), ())), preferred_element_type=F32)


def shape(dims, dtype):
    return jax.ShapeDtypeStruct(dims, dtype)


def iota(dims, axis):
    return lax.broadcasted_iota(jnp.int32, dims, axis)


def as_f32(mask):
    return jnp.where(mask, 1.0, 0.0).astype(F32)


def stack_base(rows):
    return (KS + 1) * rows


def tap_places(rows):
    width = stack_base(rows) + 256
    q = iota((KS * KS, width), 1)
    base = stack_base(rows)
    w = q % 128 + REACH
    w = jnp.where(w >= 128, w - 128, w)
    row_j = q // 128 * (128 // rows) + w // rows
    row_a = w % rows
    t = q % HALO
    halo_j = (q - base) % 128 // HALO
    upper = q >= base + 128
    halo_a = jnp.where(upper, t + REACH + 1, t - REACH)
    j = jnp.where(q < base, row_j, halo_j)
    a = jnp.where(q < base, row_a, halo_a)
    halo_ok = (upper & (t < REACH)) | ((q < base + 128) & (t >= REACH) & (t < 2 * REACH))
    ok = (j < KS) & (a < KS) & (a >= 0) & ((q < base) | halo_ok)
    return jnp.where(ok, a * KS + j, -1), upper


def split(value):
    high = value.astype(BF16)
    return high, (value - high.astype(F32)).astype(BF16)


def tap_rows(taps, rows, adjoint=None):
    place, upper = tap_places(rows)
    if adjoint is not None:
        keep = (upper & (adjoint != 0)) | (place < 0)
        place = jnp.where(keep, place, KS * KS - 1 - place)
    pick = as_f32(place == iota(place.shape, 0)).astype(BF16)
    high, low = split(taps)
    return dot(high, pick, 1, 0) + dot(low, pick, 1, 0)


def valid_rows(rows):
    q = iota((rows, stack_base(rows)), 1)
    gap = q % rows - iota((rows, stack_base(rows)), 0)
    return (gap >= -REACH) & (gap <= REACH)


def valid_halo():
    r = iota((8, 128), 0)
    q = iota((8, 128), 1)
    t = q % HALO
    inside = q < KS * HALO
    low = (r < REACH) & (t >= REACH) & (t < 2 * REACH) & inside
    up = (r >= 8 - REACH) & (t < REACH) & inside
    return low, up


def tap_matrix(row, rows):
    base = stack_base(rows)
    parts = [
        pltpu.roll(jnp.broadcast_to(row[:, v : v + 128], (rows, 128)), 0, 1, stride=1, stride_axis=0)
        for v in range(0, base, 128)
    ]
    own = jnp.where(valid_rows(rows), jnp.concatenate(parts, axis=1), 0.0)
    low_ok, up_ok = valid_halo()
    low = jnp.broadcast_to(row[:, base : base + 128], (8, 128))
    up = jnp.broadcast_to(row[:, base + 128 :], (8, 128))
    low = jnp.where(low_ok, pltpu.roll(low, 0, 1, stride=1, stride_axis=0), 0.0)
    up = jnp.where(up_ok, pltpu.roll(up, 128 - 7, 1, stride=1, stride_axis=0), 0.0)
    halo = jnp.concatenate([low, jnp.zeros((rows - 16, 128), F32), up], axis=0)
    return jnp.concatenate([own, halo], axis=1)


def tap_sums(m, rows):
    base = stack_base(rows)

    def aligned(v, shift):
        v = pltpu.roll(v, shift % 128, 1, stride=1, stride_axis=0)
        return jnp.sum(v, axis=0, keepdims=True)

    q = iota((rows, base), 1)
    gap = q % rows + iota((rows, base), 0) - (rows - 1)
    own = jnp.where((gap >= -REACH) & (gap <= REACH), m[:, :base], 0.0)
    parts = [aligned(own[:, v : v + 128], 1 - rows) for v in range(0, base, 128)]
    r = iota((8, 128), 0)
    q = iota((8, 128), 1)
    t = q % HALO
    inside = q < KS * HALO
    low_ok = (r >= 8 - REACH) & (t >= REACH) & (t < 2 * REACH) & inside
    up_ok = (r < REACH) & (t < REACH) & inside
    low = jnp.where(low_ok, m[rows - 8 :, base:], 0.0)
    up = jnp.where(up_ok, m[:8, base:], 0.0)
    return jnp.concatenate(parts + [aligned(low, -7), aligned(up, 0)], axis=1)


def shift_stack(own, edge):
    lanes = own.shape[1]
    rows = own.shape[0] - HALO
    lane = iota(own.shape, 1)
    mains, halos = [], []
    for j in range(KS):
        d = j - REACH
        if d == 0:
            s = own
        elif d > 0:
            s = pltpu.roll(jnp.where(lane < d, edge, own), lanes - d, 1)
        else:
            s = pltpu.roll(jnp.where(lane >= lanes + d, edge, own), -d, 1)
        mains.append(s[:rows].astype(BF16))
        halos.append(s[rows:])
    halos.append(jnp.zeros_like(halos[0]))
    pairs = [
        jnp.concatenate([halos[i], halos[i + 1]], axis=0).astype(BF16)
        for i in range(0, KS + 1, 2)
    ]
    gap = jnp.zeros((rows, lanes), BF16)
    rest = jnp.zeros((128 - (KS + 1) * HALO, lanes), BF16)
    return jnp.concatenate(mains + [gap] + pairs + [rest], axis=0)


def stage_halo(north, lat_ref, fold_ref, rb, rh):
    channels, lanes = lat_ref.shape[1], lat_ref.shape[2] // 2
    is_north = north != 0
    for t in range(REACH):
        near = lat_ref[t].astype(F32)
        far = fold_ref[t].astype(F32)
        up = jnp.where(is_north, far, near)
        low = jnp.where(is_north, near, jnp.zeros_like(near))
        rb[pl.ds(t * channels, channels), :] = up[:, :lanes]
        rh[pl.ds(t * channels, channels), :] = up[:, lanes:]
        rb[pl.ds((REACH + t) * channels, channels), :] = low[:, :lanes]
        rh[pl.ds((REACH + t) * channels, channels), :] = low[:, lanes:]
    for t in range(2 * REACH, HALO):
        rb[pl.ds(t * channels, channels), :] = jnp.zeros((channels, lanes), F32)
        rh[pl.ds(t * channels, channels), :] = jnp.zeros((channels, lanes), F32)


def channel_stack(c, x_ref, h_ref, rb, rh):
    at = pl.ds(c, HALO, stride=rb.shape[0] // HALO)
    own = jnp.concatenate([x_ref[c].astype(F32), rb[at, :]], axis=0)
    edge = jnp.concatenate([h_ref[c].astype(F32), rh[at, :]], axis=0)
    return shift_stack(own, edge)


def lane_edges(cells):
    lanes = cells.shape[1]
    k = iota((2 * HALO, lanes), 0)
    lane = iota((2 * HALO, lanes), 1)
    pick = ((k < REACH) & (lane == k)) | (
        (k >= HALO) & (k < HALO + REACH) & (lane == lanes - REACH + k - HALO)
    )
    return dot(as_f32(pick).astype(BF16), cells, 1, 1)


def pack_kernel(x_ref, lo_ref, hi_ref):
    edges = lane_edges(x_ref[...])
    lo_ref[...] = edges[:HALO].astype(BF16)
    hi_ref[...] = edges[HALO:].astype(BF16)


def unpack_kernel(north_ref, x_ref, east_ref, west_ref, h_ref, lat_ref, fold_ref, xs, hs):
    channels, rows, lanes = x_ref.shape
    k = iota((HALO, lanes), 0)
    lane = iota((HALO, lanes), 1)
    sel_e = as_f32((k < REACH) & (lane == k)).astype(BF16)
    sel_w = as_f32((k < REACH) & (lane == lanes - REACH + k)).astype(BF16)
    sel = jnp.concatenate([sel_e, sel_w], axis=0)
    ed = jnp.concatenate([east_ref[...], west_ref[...]], axis=0)
    hf = dot(ed, sel, 0, 0).reshape(channels, rows, lanes)
    h_ref[...] = hf.astype(BF16)
    g = HALO
    xs[0] = x_ref[:, :16, :].astype(F32)[:, :g].reshape(channels * g, lanes)
    xs[1] = x_ref[:, rows - 16 :, :].astype(F32)[:, 16 - g :].reshape(channels * g, lanes)
    hs[0] = hf[:, :g].reshape(channels * g, lanes)
    hs[1] = hf[:, rows - g :].reshape(channels * g, lanes)
    is_north = north_ref[0] != 0
    rev = as_f32(iota((lanes, lanes), 0) + iota((lanes, lanes), 1) == lanes - 1).astype(BF16)
    for t in range(REACH):
        for part, ref in ((0, xs), (1, hs)):
            bottom = ref.at[0][pl.ds(t, channels, stride=g), :]
            top = ref.at[1][pl.ds(g - REACH + t, channels, stride=g), :]
            span = slice(part * lanes, (part + 1) * lanes)
            lat_ref[t, :, span] = jnp.where(is_north, bottom, top).astype(BF16)
            fold_ref[REACH - 1 - t, :, span] = dot(top.astype(BF16), rev, 1, 0).astype(BF16)


def gelu_parts(hidden):
    k0 = 0.7978845608028654
    k1 = 0.044715 * k0
    sq = hidden * hidden
    th = jnp.tanh(hidden * (k0 + k1 * sq))
    half = 0.5 * th + 0.5
    act = hidden * half
    slope = half + act * (1.0 - th) * (k0 + 3.0 * k1 * sq)
    return act, slope


def main_kernel(
    north_ref, gain_ref, scale_ref, x_ref, h_ref, lat_ref, fold_ref, taps_ref, cot_ref, mask_ref,
    wet_ref, we_ref, wr_ref, wrt_ref,
    out_ref, g_ref, back_ref, low_ref, high_ref, keep_ref, send_ref, sums_ref,
    conv, cots, gs, gr, ms, rb, rh, act_s, hg_s, exp_ref, red_ref, rows_s, gain_s, scale_s,
):
    chunk, rows, lanes = x_ref.shape
    hiddens, channels = wet_ref.shape
    step = pl.program_id(0)

    @pl.when(step == 0)
    def _():
        rows_s[...] = tap_rows(taps_ref[...], rows)

    @pl.when(step < MAIN)
    def _():
        first = step * chunk
        stage_halo(north_ref[0], lat_ref, fold_ref, rb, rh)

        def conv_step(k, carry):
            c = first + k
            stack = channel_stack(k, x_ref, h_ref, rb, rh)
            high, low = split(tap_matrix(rows_s[pl.ds(c, 1), :], rows))
            both = dot(jnp.concatenate([high, low], axis=0), stack, 1, 0)
            conv[pl.ds(c, rows, stride=channels), :] = both[:rows] + both[rows:]
            wet = mask_ref[...].astype(F32)
            cots[pl.ds(c, rows, stride=channels), :] = cot_ref[k].astype(F32) * wet
            gain_s[pl.ds(c, 1), :] = jnp.full((1, lanes), gain_ref[c])
            scale_s[pl.ds(c, 1), :] = jnp.full((1, lanes), scale_ref[c])
            return carry

        lax.fori_loop(0, chunk, conv_step, 0, unroll=20)

    @pl.when(step == MAIN)
    def _():
        cell_work(
            north_ref, wet_ref, we_ref, wr_ref, wrt_ref, keep_ref, send_ref, sums_ref,
            conv, cots, gs, gr, ms, act_s, hg_s, exp_ref, red_ref, gain_s, scale_s, rows,
        )

    @pl.when(step > MAIN)
    def _():
        first = (step - MAIN - 1) * chunk

        def out_step(k, carry):
            at = pl.multiple_of((first + k) * PITCH, 8)
            wet = mask_ref[...].astype(F32)
            out_ref[k] = (x_ref[k].astype(F32) + wet * ms[pl.ds(at, rows), :]).astype(BF16)
            g_ref[k] = gs[pl.ds(at, rows), :].astype(BF16)
            back_ref[k] = gr[pl.ds(at, rows), :].astype(BF16)
            return carry

        lax.fori_loop(0, chunk, out_step, 0, unroll=10)
        edges = lane_edges(g_ref[...].reshape(chunk * rows, lanes))
        low_ref[...] = edges[:HALO].astype(BF16)
        high_ref[...] = edges[HALO:].astype(BF16)


def cell_work(
    north_ref, wet_ref, we_ref, wr_ref, wrt_ref, keep_ref, send_ref, sums_ref,
    conv, cots, gs, gr, ms, act_s, hg_s, exp_ref, red_ref, gain_s, scale_s, rows,
):
    hiddens, channels = wet_ref.shape
    lanes = conv.shape[1]
    exp_ref[...] = jnp.zeros_like(exp_ref)
    red_ref[...] = jnp.zeros_like(red_ref)
    sums_ref[...] = jnp.zeros_like(sums_ref)

    def cat(values):
        return jnp.concatenate(values, axis=1)

    def group(ref, i):
        at = [pl.multiple_of((WIDE * i + k) * channels, 8) for k in range(WIDE)]
        return cat([ref[pl.ds(a, channels), :] for a in at])

    def ungroup(ref, i, value):
        for k in range(WIDE):
            ref[pl.ds(WIDE * i + k, channels, stride=PITCH), :] = value[:, k * lanes : (k + 1) * lanes]

    def fold(value):
        return sum(value[:, k * lanes : (k + 1) * lanes] for k in range(WIDE))

    def cell_step(i, carry):
        gain = cat([gain_s[...]] * WIDE)
        scale = cat([scale_s[...]] * WIDE)
        value = group(conv, i)
        centred = value - jnp.mean(value, axis=0, keepdims=True)
        inverse = lax.rsqrt(jnp.mean(centred * centred, axis=0, keepdims=True) + 1e-06)
        normalized = centred * inverse
        normed = (normalized * gain).astype(BF16)
        branch = group(cots, i)
        mixed_grad = (scale * branch).astype(BF16)
        part = hiddens
        for f in range(0, hiddens, part):
            hidden = dot(wet_ref[f : f + part, :], normed, 1, 0)
            act_grad = dot(wr_ref[f : f + part, :], mixed_grad, 1, 0)
            act, slope = gelu_parts(hidden)
            act_s[f : f + part, :] = act.astype(BF16)
            hg_s[f : f + part, :] = (act_grad * slope).astype(BF16)
        mixed = dot(wrt_ref[...], act_s[...], 1, 0)
        red_ref[...] += dot(act_s[...], mixed_grad, 1, 1)
        normed_grad = dot(we_ref[...], hg_s[...], 1, 0)
        exp_ref[...] += dot(hg_s[...], normed, 1, 1)
        ungroup(ms, i, scale * mixed)
        sums_ref[1] += fold(branch * mixed)
        sums_ref[0] += fold(normed_grad * normalized)
        unit = normed_grad * gain
        m1 = jnp.mean(unit, axis=0, keepdims=True)
        m2 = jnp.mean(unit * normalized, axis=0, keepdims=True)
        grad = inverse * (unit - m1 - normalized * m2)
        ungroup(gs, i, grad)
        for k in range(WIDE):
            at = pl.ds(rows - 1 - WIDE * i - k, channels, stride=PITCH)
            gr[at, :] = grad[:, k * lanes : (k + 1) * lanes]
        return carry

    lax.fori_loop(0, rows // WIDE, cell_step, 0)
    is_north = north_ref[0] != 0
    expand, reduce = exp_ref[...], red_ref[...]
    mine = jnp.where(is_north, reduce, expand)
    theirs = jnp.where(is_north, expand, reduce)
    blank = jnp.zeros((hiddens, 2 * lanes - channels), F32)
    for ref, value in ((keep_ref, mine), (send_ref, theirs)):
        ref[:hiddens, :] = value[:, :lanes].astype(ref.dtype)
        ref[hiddens:, :] = cat([value[:, lanes:], blank]).astype(ref.dtype)


def tap_kernel(north_ref, x_ref, h_ref, lat_ref, fold_ref, back_ref, sums_ref, small_ref, rb, rh, rows_s):
    chunk, rows, lanes = x_ref.shape
    stage_halo(north_ref[0], lat_ref, fold_ref, rb, rh)

    def step(k, carry):
        stack = channel_stack(k, x_ref, h_ref, rb, rh)
        rows_s[pl.ds(k, 1), :] = tap_sums(dot(back_ref[k], stack, 1, 1), rows)
        return carry

    lax.fori_loop(0, chunk, step, 0, unroll=20)
    place, _ = tap_places(rows)
    pick = as_f32(place == iota(place.shape, 0))
    blank = jnp.zeros((SMALL - KS * KS, pick.shape[1]), F32)
    pick = jnp.concatenate([pick, blank], axis=0).astype(BF16)
    high, low = split(rows_s[...])
    taps = dot(high, pick, 1, 1) + dot(low, pick, 1, 1)
    lane = iota((chunk, SMALL), 1)
    for i in range(2):
        total = jnp.sum(sums_ref[i], axis=1, keepdims=True)
        taps = jnp.where(lane == KS * KS + i, total, taps)
    small_ref[...] = taps


def adjoint_kernel(north_ref, g_ref, h_ref, lat_ref, fold_ref, taps_ref, cot_ref, *refs):
    out_ref, rb, rh, rows_s = refs[-4:]
    chunk, rows, lanes = g_ref.shape
    stage_halo(north_ref[0], lat_ref, fold_ref, rb, rh)
    rows_s[...] = tap_rows(taps_ref[...], rows, north_ref[0])

    def step(k, carry):
        stack = channel_stack(k, g_ref, h_ref, rb, rh)
        matrix = tap_matrix(rows_s[pl.ds(k, 1), :], rows).astype(BF16)
        out_ref[k] = (cot_ref[k].astype(F32) + dot(matrix, stack, 1, 0)).astype(BF16)
        return carry

    lax.fori_loop(0, chunk, step, 0, unroll=20)


def lon_edges(low, high):
    n = lax.axis_size("lon")
    east = lax.ppermute(low, "lon", [((i + 1) % n, i) for i in range(n)])
    west = lax.ppermute(high, "lon", [(i, (i + 1) % n) for i in range(n)])
    return east, west


def halo_rows(field, east, west, north):
    channels, rows, lanes = field.shape
    n, m = lax.axis_size("lon"), lax.axis_size("lat")
    msg = shape((REACH, channels, 2 * lanes), BF16)
    lane_halo, lat_msg, fold_msg = call(
        unpack_kernel,
        (shape(field.shape, BF16), msg, msg),
        scratch=[pltpu.VMEM((2, channels * HALO, lanes), F32)] * 2,
        n_smem=1,
        n_in=4,
        cost=cost(3),
    )(north, field, east, west)
    fold_rows = lax.ppermute(
        fold_msg, ("lon", "lat"), [(i * m + m - 1, (n - 1 - i) * m + m - 1) for i in range(n)]
    )
    lat_rows = lax.ppermute(lat_msg, "lat", [(0, 1), (1, 0)])
    return lane_halo, lat_rows, fold_rows


def cost(micros):
    return pl.CostEstimate(flops=int(micros * 1e9), bytes_accessed=int(micros * 3e6), transcendentals=0)


def halves(buf, bit):
    half = buf.shape[0] // 2
    first, second = buf[:half], buf[half:]
    up = bit != 0
    return jnp.where(up, second, first), jnp.where(up, first, second)


def joined(mine, other, bit):
    up = bit != 0
    return jnp.concatenate([jnp.where(up, other, mine), jnp.where(up, mine, other)], axis=0)


def partner(value, axis, b):
    return lax.ppermute(value, axis, [(i, i ^ (1 << b)) for i in range(lax.axis_size(axis))])


def lon_bits():
    return range(lax.axis_size("lon").bit_length() - 1)


def together(*values):
    return lax.optimization_barrier(values)


def on_device(
    ocean_state, cotangent, kernel, norm_gain, expand_weight, reduce_weight, layer_scale, land_mask
):
    channels, rows, lanes = ocean_state.shape
    hiddens = expand_weight.shape[1]
    width = stack_base(rows) + 256
    is_north = lax.axis_index("lat") == lax.axis_size("lat") - 1
    north = is_north.astype(jnp.int32).reshape(1)
    edge = shape((HALO, channels * rows), BF16)
    field = shape(ocean_state.shape, BF16)
    rowbuf = pltpu.VMEM((HALO * (channels // CHUNKS), lanes), F32)
    cellbuf = pltpu.VMEM((channels * rows, lanes), F32)
    pitchbuf = pltpu.VMEM((channels * PITCH, lanes), F32)
    tapbuf = pltpu.VMEM((channels, width), F32)
    hidbuf = pltpu.VMEM((hiddens, WIDE * lanes), BF16)
    gradbuf = pltpu.VMEM((hiddens, channels), F32)
    lanebuf = pltpu.VMEM((channels, lanes), F32)

    low, high = call(pack_kernel, (edge, edge), n_in=1, cost=cost(2))(
        ocean_state.reshape(channels * rows, lanes)
    )
    east, west = lon_edges(low, high)
    halo, lat_rows, fold_rows = halo_rows(ocean_state, east, west, north)

    chunk = channels // CHUNKS
    whole = vmem()

    big = channels // MAIN

    def block(index, size=chunk):
        return pl.BlockSpec((size, rows, lanes), lambda i: (index(i), 0, 0))

    def into(i):
        return jnp.minimum(i, MAIN - 1)

    def back_out(i):
        return jnp.maximum(i - MAIN - 1, 0)

    def both_ways(i):
        return jnp.where(i <= MAIN, into(i), back_out(i))

    def halo_block(index, size=chunk):
        return pl.BlockSpec((REACH, size, 2 * lanes), lambda i: (0, index(i), 0))

    edge_block = pl.BlockSpec((HALO, big * rows), lambda i: (0, back_out(i)))
    block_out, conv_grad, back_grad, g_low, g_high, keep, send, sums = grid_call(
        main_kernel,
        2 * MAIN + 1,
        (
            field,
            field,
            field,
            edge,
            edge,
            shape((2 * hiddens, lanes), F32),
            shape((2 * hiddens, lanes), BF16),
            shape((2, channels, lanes), F32),
        ),
        [smem()] * 3 + [block(both_ways, big), block(into, big)] + [halo_block(into, big)] * 2
        + [whole, block(into, big)] + [whole] * 5,
        [block(back_out, big)] * 3 + [edge_block] * 2 + [whole] * 3,
        [cellbuf] * 2 + [pitchbuf] * 3 + [pltpu.VMEM((HALO * big, lanes), F32)] * 2 + [hidbuf] * 2 + [gradbuf] * 2 + [tapbuf] + [lanebuf] * 2,
        cost(40),
    )(
        north, norm_gain, layer_scale, ocean_state, halo, lat_rows, fold_rows, kernel, cotangent, land_mask,
         expand_weight.T, expand_weight, reduce_weight, reduce_weight.T,
    )

    def adjoint_part(start, count, grad, lane_halo, previous):
        here, rows_in = block(lambda i: i + start), halo_block(lambda i: i + start)
        extra = () if previous is None else (previous,)
        return grid_call(
            adjoint_kernel,
            count,
            field,
            [smem(), here, here, rows_in, rows_in]
            + [pl.BlockSpec((chunk, KS * KS), lambda i: (i + start, 0)), here]
            + [pl.BlockSpec(memory_space=pl.ANY)] * len(extra),
            here,
            [rowbuf] * 2 + [pltpu.VMEM((chunk, width), F32)],
            cost(2 * count),
            {7: 0} if extra else None,
        )(north, grad, lane_halo, g_lat, g_fold, kernel, cotangent, *extra)

    g_east, g_west = lon_edges(g_low, g_high)
    def taps_part(start, count, back):
        here, rows_in = block(lambda i: i + start), halo_block(lambda i: i + start)
        return grid_call(
            tap_kernel,
            count,
            shape((count * chunk, SMALL), F32),
            [smem(), here, here, rows_in, rows_in]
            + [here, pl.BlockSpec((2, chunk, lanes), lambda i: (0, i + start, 0))],
            pl.BlockSpec((chunk, SMALL), lambda i: (i, 0)),
            [rowbuf] * 2 + [pltpu.VMEM((chunk, width), F32)],
            cost(3 * count),
        )(north, ocean_state, halo, lat_rows, fold_rows, back, sums)

    buf = keep + partner(send, "lat", 0).astype(F32)
    bits = list(lon_bits())
    parts, taps_done, back = [], 0, back_grad
    g_halo, state_grad, done, grad = None, None, 0, conv_grad
    steps = [(b, True) for b in bits] + [(b, False) for b in bits[::-1]]
    for b, halving in steps:
        bit = (lax.axis_index("lon") >> b) & 1
        if halving:
            stay, go = halves(buf, bit)
            go = go.astype(BF16)
        else:
            if done == 0:
                small = jnp.concatenate(parts, axis=0)
                half = channels // 2
                small = jnp.concatenate([small[:half], small[half:]], axis=1)
                small = jnp.pad(small, ((0, -half % 8), (0, 0)))
                small = small + partner(small, "lat", 0)
            stay, own = buf.astype(BF16), small.astype(BF16)
            go = jnp.concatenate([stay, own], axis=0)
        go, grad, back = together(go, grad, back)
        got = partner(go, "lon", b)
        if taps_done and g_halo is None:
            g_halo, g_lat, g_fold = halo_rows(grad, g_east, g_west, north)
            got, g_halo, back = together(got, g_halo, back)
        elif taps_done < CHUNKS:
            count = min(CHUNKS - taps_done, (CHUNKS + 1) // 2)
            parts.append(taps_part(taps_done, count, back))
            taps_done += count
            got, parts[-1] = together(got, parts[-1])
        elif done < CHUNKS and not halving:
            count = min(2, CHUNKS - done)
            state_grad = adjoint_part(done, count, grad, g_halo, state_grad)
            done += count
            got, state_grad = together(got, state_grad)
        if halving:
            buf = stay + got.astype(F32)
        else:
            rows_here = stay.shape[0]
            buf = joined(stay, got[:rows_here], bit)
            small = own.astype(F32) + got[rows_here:].astype(F32)
    if done < CHUNKS:
        state_grad = adjoint_part(done, CHUNKS - done, grad, g_halo, state_grad)
    other = partner(buf, "lat", 0)

    def unfolded(value):
        top, rest = value[:hiddens], value[hiddens:, : channels - lanes]
        return jnp.concatenate([top, rest], axis=1).astype(F32)

    expand = unfolded(jnp.where(is_north, other, buf))
    reduce = unfolded(jnp.where(is_north, buf, other))
    half = channels // 2
    small = jnp.concatenate([small[:half, :SMALL], small[:half, SMALL:]], axis=0)
    kernel_grad = small[:, : KS * KS]
    gain_grad = small[:, KS * KS]
    scale_grad = small[:, KS * KS + 1]
    return (block_out, state_grad, kernel_grad, gain_grad, expand.T, reduce, scale_grad)


def solution(mesh):
    tiles = P(None, ("members", "lat"), "lon")
    return jax.shard_map(
        on_device,
        mesh=mesh,
        in_specs=(tiles, tiles, P(), P(), P(), P(), P(), P("lat", "lon")),
        out_specs=(
            tiles, tiles, P("members", None), P("members"), P("members", None),
            P("members", None), P("members"),
        ),
        check_vma=False,
    )
```
